128 devices in a mesh: grp: 4 (over x), patch: 32 (over z, y, core).
Axes of the slice: x: 4, y: 4, z: 4, core: 2. Of those that a mesh axis runs over, the one named last changes fastest.
Arguments:
- forcing: bfloat16 [4, 1024, 192, 128], P('grp', 'patch'), may hold values from -6 to 6
- stiffness: float32 [4, 1024, 128], P('grp', 'patch'), may hold values from 0.5 to 5
- reaction: float32 [4, 1024, 128], P('grp', 'patch'), may hold values from 0.02 to 0.2
- volumetric: float32 [4, 1024, 128], P('grp', 'patch'), may hold values from 0.2 to 2
- adjacency: int32 [128, 26], replicated, may hold values from 0 to 127
- owner_map: int32 [128, 26], replicated, may hold values from 0 to 31, as said below
- param_scale: float32 [512, 128], replicated, may hold values from 0.25 to 4
- coefficients: float32 [512, 64], replicated, may hold values from -6 to 6
Outputs:
- basis: bfloat16 [4, 1024, 192, 128], P('grp', 'patch')
- block_norms: float32 [32, 512, 256], P('patch', 'grp')
- estimate: float32 [512], P('grp')
The draws below stay inside these ranges and needn't reach their ends.
Inputs may be any that keep to these rules, and one draw needn't show every extreme that they name: `owner_map`: no subdomain has more than 2 blocks with one owner, and the blocks of one subdomain with one owner stand in consecutive slots; in each group some owner gets exactly 2 blocks from every subdomain of the group.
All inputs are finite; a program needn't handle non-finite values.
Results may differ from the reference program's by a relative error of at most 0.0045.
Values may be sent and summed in bfloat16 or wider, within the bound.
A program may use at most 64 MiB of HBM per device.

```python
import math
import jax
import jax.numpy as jnp
from jax import lax

K = 64
P_SIZE = 512
NBR = 26
ITERS = 8
CX = 32
CZ = 128
KC = 192
SUB = 128
SCAP = 2
SLOTS = 256
N_GRP = 4
N_PATCH = 32


def draw_owner_map(key, part):
    keys = jax.random.split(jax.random.fold_in(key, 7), SUB + 1)
    groups = SUB // N_PATCH
    special = jax.random.randint(keys[0], (groups,), 0, N_PATCH)
    orders = jax.vmap(lambda single: jax.random.permutation(single, N_PATCH))(keys[1:])
    target = special[jnp.arange(SUB) // N_PATCH]
    leading = orders[:, 0]
    swapped = jnp.where(orders == target[:, None], leading[:, None], orders)
    swapped = swapped.at[:, 0].set(target)
    columns = jnp.arange(NBR) // SCAP
    return swapped[:, columns].astype(jnp.int32)


def with_ends(entries, key, least, largest):
    spot = [jax.random.randint(jax.random.fold_in(key, axis), (), 0, length) for axis, length in enumerate(entries.shape)]
    main_axis = entries.shape.index(max(entries.shape))
    neighbour = spot[:main_axis] + [(spot[main_axis] + 1) % entries.shape[main_axis]] + spot[main_axis + 1:]
    return entries.at[tuple(spot)].set(least).at[tuple(neighbour)].set(largest)


def shard_levels(key, extent, shards, smallest, high):
    def one(position, blocks):
        steps = jax.random.uniform(jax.random.fold_in(jax.random.fold_in(key, 6), position), (blocks,), jnp.float32, smallest / len(shards), high / len(shards))
        return jnp.repeat(jnp.exp(steps), extent[position] // blocks).reshape((-1,) + (1,) * (len(extent) - position - 1))

    level = one(*shards[0])
    for cut in shards[1:]:
        level = level * one(*cut)
    return level


def scatter_about(key, shape, spread, reach, cuts=(), kind=jnp.bfloat16):
    gain = shard_levels(key, shape, cuts, -0.22, 0.18) if cuts else 1.0
    drawn = jax.random.normal(key, shape, jnp.float32) * spread * gain
    return jnp.minimum(jnp.maximum(drawn, -reach), reach).astype(kind)


def setup_inputs(seed: int = 0) -> dict:
    key_list = jax.random.split(jax.random.key(seed), 9)
    forcing = scatter_about(key_list[0], (N_GRP, N_PATCH * CX, KC, CZ), 1.0, 6.0, ((0, 4), (1, 32)))
    stiffness = jnp.clip(jnp.exp(math.log(5.0) - 2.3025851 * jax.random.uniform(key_list[1], (N_GRP, N_PATCH * CX, CZ), jnp.float32) ** shard_levels(key_list[1], (N_GRP, N_PATCH * CX, CZ), ((0, 4), (1, 32)), -0.2, 0.2)), 0.5, 5.0)
    reaction = jnp.clip(jnp.exp(math.log(0.2) - 2.3025851 * jax.random.uniform(key_list[2], (N_GRP, N_PATCH * CX, CZ), jnp.float32) ** shard_levels(key_list[2], (N_GRP, N_PATCH * CX, CZ), ((0, 4), (1, 32)), -0.2, 0.2)), 0.02, 0.2)
    volumetric = jnp.clip(jnp.exp(math.log(2.0) - 2.3025851 * jax.random.uniform(key_list[3], (N_GRP, N_PATCH * CX, CZ), jnp.float32) ** shard_levels(key_list[3], (N_GRP, N_PATCH * CX, CZ), ((0, 4), (1, 32)), -0.2, 0.2)), 0.2, 2.0)
    adjacency = with_ends(jax.random.randint(key_list[4], (SUB, NBR), 0, SUB), jax.random.fold_in(key_list[4], 1), 0, SUB - 1).astype(jnp.int32)
    owner_map = draw_owner_map(jax.random.fold_in(key_list[8], 71), 0)
    param_scale = jnp.clip(jnp.exp(jax.random.uniform(key_list[6], (P_SIZE, SUB), jnp.float32, math.log(0.25), math.log(4.0))), 0.25, 4.0)
    coefficients = scatter_about(key_list[7], (P_SIZE, K), 1.0, 6.0, (), jnp.float32)
    return {"forcing": forcing, "stiffness": stiffness, "reaction": reaction, "volumetric": volumetric, "adjacency": adjacency, "owner_map": owner_map, "param_scale": param_scale, "coefficients": coefficients}


OMEGA = 0.8
EPS = 1e-06

def stencil(padded, stiff_pad, reaction, volumetric):
    values = padded[1:-1]
    stiff_mid = stiff_pad[1:-1]
    west_face = 0.5 * (stiff_mid + stiff_pad[:-2])
    east_face = 0.5 * (stiff_mid + stiff_pad[2:])
    stiff_side = jnp.pad(stiff_mid, ((0, 0), (1, 1)))
    south_face = 0.5 * (stiff_mid + stiff_side[:, :-2])
    north_face = 0.5 * (stiff_mid + stiff_side[:, 2:])
    values_side = jnp.pad(values, ((0, 0), (0, 0), (1, 1)))
    length, channels, cells_z = values.shape
    grouped = values.reshape(length, channels // 3, 3, cells_z)
    summed = jnp.broadcast_to(lax.optimization_barrier(jnp.sum(grouped, axis=2, keepdims=True)), grouped.shape).reshape(values.shape)
    diagonal = reaction + west_face + east_face + south_face + north_face + volumetric
    beside = west_face[:, None] * padded[:-2] + east_face[:, None] * padded[2:] + south_face[:, None] * values_side[:, :, :-2] + north_face[:, None] * values_side[:, :, 2:]
    applied = (diagonal - volumetric)[:, None] * values + volumetric[:, None] * summed - beside
    return (applied, diagonal)

def relax(values, padded, stiff_pad, reaction, volumetric, loads):
    applied, diagonal = stencil(padded, stiff_pad, reaction, volumetric)
    return values + OMEGA * (loads - applied) / diagonal[:, None]

def ranks(owners):
    count = owners.shape[-1]
    same = owners[:, :, None] == owners[:, None, :]
    before = jnp.arange(count, dtype=jnp.int32)[None, :] < jnp.arange(count, dtype=jnp.int32)[:, None]
    return lax.optimization_barrier(jnp.sum((same & before[None]).astype(jnp.int32), axis=2)).astype(jnp.int32)

def residual_squares(blocks, coeffs, scale_src, scale_nbr):
    forward = jnp.einsum('bkl,pl->pbk', blocks, coeffs, precision=lax.Precision.HIGHEST)
    backward = jnp.einsum('blk,pl->pbk', blocks, coeffs, precision=lax.Precision.HIGHEST)
    residual = scale_src[:, :, None] * forward - scale_nbr[:, :, None] * backward
    return lax.optimization_barrier(jnp.sum(residual * residual, axis=2))

def group_basis(inputs):
    loads, stiff_grid, react_grid, volume_grid = inputs
    loads = loads.astype(jnp.float32)
    values = jnp.zeros(loads.shape, jnp.float32)
    stiff_pad = jnp.pad(stiff_grid, ((1, 1), (0, 0)))
    for repeat in range(ITERS):
        padded = jnp.pad(values, ((1, 1), (0, 0), (0, 0)))
        values = relax(values, padded, stiff_pad, react_grid, volume_grid, loads)
    return values.astype(jnp.bfloat16)

def reference(forcing, stiffness, reaction, volumetric, adjacency, owner_map, param_scale, coefficients):
    basis = lax.map(group_basis, (forcing, stiffness, reaction, volumetric))
    traces = basis.reshape(N_GRP, N_PATCH, CX, K, 3, CZ)[:, :, CX - 1, :, 0, :].reshape(SUB, K, CZ)
    weights = stiffness.reshape(N_GRP, N_PATCH, CX, CZ)[:, :, CX - 1, :].reshape(SUB, CZ)
    scaled = (traces.astype(jnp.float32) * weights[:, None, :]).astype(jnp.bfloat16)

    def per_subdomain(index):
        partners = adjacency[index]
        partner_traces = traces[partners].astype(jnp.float32)
        blocks = jnp.einsum('kz,slz->skl', scaled[index].astype(jnp.float32), partner_traces, precision=lax.Precision.HIGHEST)
        scale_src = jnp.broadcast_to(param_scale[:, index][:, None], (P_SIZE, NBR))
        scale_nbr = param_scale[:, partners]
        return residual_squares(blocks, coefficients, scale_src, scale_nbr)
    squares_all = lax.map(per_subdomain, jnp.arange(SUB, dtype=jnp.int32))
    rank = ranks(owner_map)
    column = jnp.arange(SUB, dtype=jnp.int32)[:, None] * SCAP + rank
    table = jnp.zeros((N_PATCH, P_SIZE, SLOTS), jnp.float32)
    table = table.at[owner_map.reshape(-1), :, column.reshape(-1)].set(jnp.transpose(squares_all, (0, 2, 1)).reshape(SUB * NBR, P_SIZE))
    block_norms = jnp.sqrt(table + EPS)
    estimate = jnp.sqrt(lax.optimization_barrier(jnp.sum(table, axis=(0, 2))) + EPS)
    return (basis, block_norms, estimate)
```

```python
import jax
import jax.numpy as jnp
from jax import lax
from jax.experimental import pallas as pl
from jax.experimental.pallas import tpu as pltpu
from jax.sharding import PartitionSpec as P

MESH = pl.DeviceIdType.MESH
OMEGA = 0.8
EPS = 1e-06
ROWS = 32
K = 64
Z = 128
HALO = 7
VMEM_LIMIT = 62 * 1024 * 1024


def position(i):
    core = i & 1
    y = (i >> 1) & 3
    z = (i >> 3) & 3
    x = i >> 5
    last = jnp.where(core == 0, z, y)
    first = jnp.where(core == 0, y, z)
    return core * 64 + last * 16 + x * 4 + first


def relax_kernel(
    f_hbm, s_hbm, r_hbm, v_hbm,
    basis_hbm, traces_hbm, rows_hbm,
    fext, cells, small, coef, u, spread, out, traces, rows,
    local_sem, halo_send, halo_recv, t_send, t_recv, r_send, r_recv, tp_send, tp_recv, rp_send, rp_recv, out_sem,
):
    x = lax.axis_index("grp")
    p = lax.axis_index("patch")
    c = p % 2
    y = (p // 2) % 4
    z = p // 8
    a = jnp.where(c == 0, z, y)
    b = jnp.where(c == 0, y, z)
    npatch = 32
    right = (p + 1) % npatch
    left = (p + npatch - 1) % npatch
    partner = p + 1 - 2 * c

    def patch_of(last, first):
        return last * (8 - 6 * c) + first * (2 + 6 * c) + c

    firsts = [(x, patch_of(a, (b + d) % 4)) for d in (1, 2, 3)]
    grps = [((x + d) % 4, p) for d in (1, 2, 3)]
    lasts = [(x, patch_of((a + d) % 4, b)) for d in (1, 2, 3)]
    other = (x, partner)

    own_f = pltpu.make_async_copy(f_hbm, fext.at[pl.ds(8, ROWS)], local_sem.at[0])
    own_cells = [
        pltpu.make_async_copy(ref, cells.at[n, pl.ds(8, ROWS)], local_sem.at[1 + n])
        for n, ref in enumerate((s_hbm, r_hbm, v_hbm))
    ]
    own_row = pltpu.make_async_copy(s_hbm.at[pl.ds(ROWS - 1, 1)], rows.at[c, a, x, b], local_sem.at[4])
    for copy in own_cells:
        copy.start()
    own_f.start()
    own_row.start()

    barrier = pltpu.get_barrier_semaphore()
    peers = [(x, left), (x, right)] + firsts + grps + lasts + [other]
    for peer in peers:
        pl.semaphore_signal(barrier, inc=1, device_id=peer, device_id_type=MESH)
    pl.semaphore_wait(barrier, len(peers))

    def remote(src, dst, ssem, rsem, device):
        return pltpu.make_async_remote_copy(
            src_ref=src, dst_ref=dst, send_sem=ssem, recv_sem=rsem, device_id=device, device_id_type=MESH
        )

    to_left, to_right = [], []
    for n, ref in enumerate((s_hbm, r_hbm, v_hbm)):
        to_left.append(
            remote(ref.at[pl.ds(0, 8)], cells.at[n, pl.ds(8 + ROWS, 8)], halo_send.at[0, n], halo_recv.at[0, n], (x, left))
        )
        to_right.append(
            remote(ref.at[pl.ds(ROWS - 8, 8)], cells.at[n, pl.ds(0, 8)], halo_send.at[1, n], halo_recv.at[1, n], (x, right))
        )
    to_left.append(
        remote(f_hbm.at[pl.ds(0, HALO)], fext.at[pl.ds(8 + ROWS, HALO)], halo_send.at[0, 3], halo_recv.at[0, 3], (x, left))
    )
    to_right.append(
        remote(f_hbm.at[pl.ds(ROWS - HALO, HALO)], fext.at[pl.ds(8 - HALO, HALO)], halo_send.at[1, 3], halo_recv.at[1, 3], (x, right))
    )
    for copy in to_left:
        copy.start()
    for copy in to_right:
        copy.start()

    def stage1(buf, ssem, rsem):
        return [remote(buf.at[c, a, x, b], buf.at[c, a, x, b], ssem.at[0, n], rsem.at[0, n], dev) for n, dev in enumerate(firsts)]

    def stage2(buf, ssem, rsem):
        return [remote(buf.at[c, a, x], buf.at[c, a, x], ssem.at[1, n], rsem.at[1, n], dev) for n, dev in enumerate(grps)]

    def stage3(buf, ssem, rsem):
        return [remote(buf.at[c, a], buf.at[c, a], ssem.at[2, n], rsem.at[2, n], dev) for n, dev in enumerate(lasts)]

    def start(copies):
        for copy in copies:
            copy.start()

    own_row.wait()
    r1 = stage1(rows, r_send, r_recv)
    start(r1)

    lane = lax.broadcasted_iota(jnp.int32, (8, Z), 1)
    sub = lax.broadcasted_iota(jnp.int32, (8, Z), 0)

    def coefficients(e0):
        mid = cells[0, pl.ds(e0, 8), :]
        row = sub + e0
        keep_w = jnp.where((row == 8) & (p == 0), 0.0, 1.0)
        keep_e = jnp.where((row == 7 + ROWS) & (p == npatch - 1), 0.0, 1.0)
        keep_s = jnp.where(lane == 0, 0.0, 1.0)
        keep_n = jnp.where(lane == Z - 1, 0.0, 1.0)
        west = 0.5 * (mid + keep_w * cells[0, pl.ds(e0 - 1, 8), :])
        east = 0.5 * (mid + keep_e * cells[0, pl.ds(e0 + 1, 8), :])
        south = 0.5 * (mid + keep_s * pltpu.roll(mid, 1, 1))
        north = 0.5 * (mid + keep_n * pltpu.roll(mid, Z - 1, 1))
        volume = cells[2, pl.ds(e0, 8), :]
        rest = cells[1, pl.ds(e0, 8), :] + west + east + south + north
        diagonal = rest + volume
        weight = OMEGA / diagonal
        values = (
            1.0 - weight * rest,
            1.0 - weight * (rest + 3.0 * volume),
            weight * west * keep_w,
            weight * east * keep_e,
            weight * south * keep_s,
            weight * north * keep_n,
            weight * (1.0 / 3.0),
        )
        for n, value in enumerate(values):
            small[n] = value
        for n in range(7):
            for k in range(8):
                coef[n, e0 + k] = jnp.broadcast_to(small[n, pl.ds(k, 1), :], (8, Z))

    def first_level(e, slot):
        spread[slot] = fext[e].astype(jnp.float32)
        parts = [spread[slot, pl.ds(n, K, stride=3), :].reshape(8, 8, Z) for n in range(3)]
        weight = coef[6, e][None]
        total = parts[0] + parts[1] + parts[2]
        u[0, e, 0:8] = weight * total
        u[0, e, 8:16] = weight * (3.0 * parts[0] - total)
        u[0, e, 16:24] = weight * (3.0 * parts[1] - total)

    def turned(value, shift):
        return pltpu.roll(value.reshape(K, Z), shift, 1).reshape(8, 8, Z)

    def update(level, e, m, before, now, after):
        centre = coef[1 if m == 0 else 0, e][None]
        return (
            u[0, e, pl.ds(8 * m, 8)]
            + centre * now
            + coef[2, e][None] * before
            + coef[3, e][None] * after
            + coef[4, e][None] * turned(now, 1)
            + coef[5, e][None] * turned(now, Z - 1)
        )

    def sweep(level, e0, n):
        for m in range(3):
            part = pl.ds(8 * m, 8)
            before = u[level - 2, e0 - 1, part]
            now = u[level - 2, e0, part]
            for k in range(n):
                after = u[level - 2, e0 + k + 1, part]
                u[level - 1, e0 + k, part] = update(level, e0 + k, m, before, now, after)
                before, now = now, after

    def last_modes(e, count):
        result = []
        for m in range(count):
            part = pl.ds(8 * m, 8)
            result.append(update(8, e, m, u[6, e - 1, part], u[6, e, part], u[6, e + 1, part]))
        return result

    def emit(e, slot):
        total, first, second = last_modes(e, 3)
        values = (total + first, total + second, total - first - second)
        for n, value in enumerate(values):
            spread[slot, pl.ds(n, K, stride=3), :] = value.reshape(K, Z)
        out[e - 8] = spread[slot].astype(jnp.bfloat16)

    for copy in own_cells:
        copy.wait()
    for e0 in (9, 17, 25, 31):
        coefficients(e0)
    own_f.wait()

    def pair_first(i, carry):
        first_level(9 + 2 * i, 0)
        first_level(10 + 2 * i, 1)
        return carry

    lax.fori_loop(0, 15, pair_first, 0)
    for level in range(2, 8):

        def pair(i, carry, level=level):
            sweep(level, 8 + level + 2 * i, 2)
            return carry

        lax.fori_loop(0, 16 - level, pair, 0)

    def finish(copies):
        for copy in copies:
            copy.wait_recv()

    finish(r1)
    r2 = stage2(rows, r_send, r_recv)
    start(r2)

    finish(to_left)
    coefficients(39)

    def right_first(i, carry):
        first_level(39 + 2 * i, 0)
        first_level(40 + 2 * i, 1)
        return carry

    lax.fori_loop(0, 4, right_first, 0)

    def right_level(level, carry):
        sweep(level, 40 - level, 8)
        return carry

    lax.fori_loop(2, 8, right_level, 0)
    total, first = last_modes(7 + ROWS, 2)
    traces[c, a, x, b] = (total + first).reshape(K, Z).astype(jnp.bfloat16)
    finish(r2)
    r3 = stage3(rows, r_send, r_recv)
    start(r3)
    t1 = stage1(traces, t_send, t_recv)
    start(t1)

    finish(to_right)
    coefficients(1)

    def left_first(i, carry):
        first_level(1 + 2 * i, 0)
        first_level(2 + 2 * i, 1)
        return carry

    lax.fori_loop(0, 4, left_first, 0)

    def left_level(level, carry):
        sweep(level, level, 8)
        return carry

    lax.fori_loop(2, 8, left_level, 0)

    finish(t1)
    t2 = stage2(traces, t_send, t_recv)
    start(t2)
    finish(r3)
    rp = remote(rows.at[c], rows.at[c], rp_send, rp_recv, other)
    rp.start()

    def pair_emit(i, carry):
        emit(8 + 2 * i, 0)
        emit(9 + 2 * i, 1)
        return carry

    half = ROWS // 2
    lax.fori_loop(0, half // 2, pair_emit, 0)
    out0 = pltpu.make_async_copy(out.at[pl.ds(0, half)], basis_hbm.at[pl.ds(0, half)], out_sem.at[0])
    out0.start()

    finish(t2)
    t3 = stage3(traces, t_send, t_recv)
    start(t3)

    def slab(k):
        where = (a + 4 - k) % 4
        return remote(traces.at[c, where], traces.at[c, where], tp_send.at[k], tp_recv.at[k], other)

    tp = [slab(k) for k in range(4)]
    tp[0].start()

    lax.fori_loop(half // 2, half, pair_emit, 0)
    out1 = pltpu.make_async_copy(out.at[pl.ds(half, half)], basis_hbm.at[pl.ds(half, half)], out_sem.at[1])
    out1.start()

    for n in (0, 2, 1):
        t3[n].wait_recv()
        tp[n + 1].start()
    finish(tp)
    rp.wait_recv()
    t_out = pltpu.make_async_copy(traces, traces_hbm, out_sem.at[2])
    t_out.start()
    r_out = pltpu.make_async_copy(rows, rows_hbm, out_sem.at[3])
    r_out.start()
    for copy in to_left + to_right + r1 + r2 + r3 + [rp] + t1 + t2 + t3 + tp:
        copy.wait_send()
    for copy in (out0, out1, t_out, r_out):
        copy.wait()


def residual_kernel(table, traces, rows, coeffs_hbm, scales_hbm, norms, partial, coeffs, scales, scales_t, squares, sem):
    g = lax.axis_index("grp")
    quarter = norms.shape[0]
    first = pltpu.make_async_copy(coeffs_hbm.at[pl.ds(g * quarter, quarter)], coeffs, sem.at[0])
    second = pltpu.make_async_copy(scales_hbm.at[pl.ds(g * quarter, quarter)], scales, sem.at[1])
    first.start()
    second.start()
    first.wait()
    second.wait()
    scales_t[...] = scales[...].T
    weights = coeffs[...].astype(jnp.bfloat16)
    contract = (((1,), (1,)), ((), ()))

    def one(i, carry):
        where = position(i)
        scaled = (traces[where].astype(jnp.float32) * rows[where]).astype(jnp.bfloat16)
        own = scales_t[pl.ds(i, 1), :]
        for k in range(2):
            entry = table[2 * i + k]
            j = jnp.maximum(entry, 0)
            live = jnp.where(entry >= 0, 1.0, 0.0).astype(jnp.float32)
            other = traces[position(j)]
            block = lax.dot_general(scaled, other, contract, preferred_element_type=jnp.float32)
            turned = lax.dot_general(other, scaled, contract, preferred_element_type=jnp.float32)
            forward = lax.dot_general(block.astype(jnp.bfloat16), weights, contract, preferred_element_type=jnp.float32)
            backward = lax.dot_general(turned.astype(jnp.bfloat16), weights, contract, preferred_element_type=jnp.float32)
            residual = own * forward - scales_t[pl.ds(j, 1), :] * backward
            squares[pl.ds(2 * i + k, 1), :] = jnp.sum(residual * residual, axis=0, keepdims=True) * live
        return carry

    lax.fori_loop(0, traces.shape[0], one, 0)
    every = squares[...]
    partial[...] = jnp.sum(every, axis=0, keepdims=True)
    norms[...] = jnp.sqrt(every.T + EPS)


def total_kernel(mine, total, inbox, send_sem, recv_sem, own_sem):
    x = lax.axis_index("grp")
    p = lax.axis_index("patch")
    count = inbox.shape[0]
    own = pltpu.make_async_copy(mine, inbox.at[p], own_sem)
    own.start()
    barrier = pltpu.get_barrier_semaphore()
    for d in range(1, count):
        pl.semaphore_signal(barrier, inc=1, device_id=(x, (p + d) % count), device_id_type=MESH)
    pl.semaphore_wait(barrier, count - 1)
    copies = []
    for d in range(1, count):
        copies.append(
            pltpu.make_async_remote_copy(
                src_ref=mine, dst_ref=inbox.at[p], send_sem=send_sem.at[d - 1], recv_sem=recv_sem.at[d - 1],
                device_id=(x, (p + d) % count), device_id_type=MESH,
            )
        )
    for copy in copies:
        copy.start()
    own.wait()
    for copy in copies:
        copy.wait_recv()
    value = inbox[0]
    for d in range(1, count):
        value = value + inbox[d]
    total[...] = value
    for copy in copies:
        copy.wait_send()


def owned(owner_map, adjacency, owner):
    mine = owner_map == owner
    earlier = jnp.pad(mine, ((0, 0), (1, 0)))[:, :-1]
    picked = jnp.stack([mine & ~earlier, mine & earlier], axis=1)
    found = jnp.sum(jnp.where(picked, adjacency[:, None, :] + 1, 0), axis=2)
    return (found - 1).reshape(-1)


def body(forcing, stiffness, reaction, volumetric, adjacency, owner_map, param_scale, coefficients):
    anywhere = pl.BlockSpec(memory_space=pl.ANY)
    vmem = pl.BlockSpec(memory_space=pltpu.VMEM)
    dma = pltpu.SemaphoreType.DMA
    f32, bf16 = jnp.float32, jnp.bfloat16
    params = pltpu.CompilerParams(collective_id=0, has_side_effects=True, vmem_limit_bytes=VMEM_LIMIT)
    basis, traces, rows = pl.pallas_call(
        relax_kernel,
        name="relax",
        out_shape=(
            jax.ShapeDtypeStruct((ROWS, 3 * K, Z), bf16),
            jax.ShapeDtypeStruct((2, 4, 4, 4, K, Z), bf16),
            jax.ShapeDtypeStruct((2, 4, 4, 4, 1, Z), f32),
        ),
        in_specs=[anywhere] * 4,
        out_specs=(anywhere,) * 3,
        scratch_shapes=[
            pltpu.VMEM((48, 3 * K, Z), bf16),
            pltpu.VMEM((3, 48, Z), f32),
            pltpu.VMEM((7, 8, Z), f32),
            pltpu.VMEM((7, 48, 8, Z), f32),
            pltpu.VMEM((7, 48, 24, 8, Z), f32),
            pltpu.VMEM((2, 3 * K, Z), f32),
            pltpu.VMEM((ROWS, 3 * K, Z), bf16),
            pltpu.VMEM((2, 4, 4, 4, K, Z), bf16),
            pltpu.VMEM((2, 4, 4, 4, 1, Z), f32),
            dma((5,)),
            dma((2, 4)),
            dma((2, 4)),
            dma((3, 3)),
            dma((3, 3)),
            dma((3, 3)),
            dma((3, 3)),
            dma((4,)),
            dma((4,)),
            dma,
            dma,
            dma((4,)),
        ],
        compiler_params=params,
    )(forcing[0], stiffness[0], reaction[0], volumetric[0])

    patch = lax.axis_index("patch")
    table = owned(owner_map, adjacency, patch)
    quarter = param_scale.shape[0] // 4
    slots = table.shape[0]
    norms, partial = pl.pallas_call(
        residual_kernel,
        name="residual",
        out_shape=(jax.ShapeDtypeStruct((quarter, slots), f32), jax.ShapeDtypeStruct((1, quarter), f32)),
        in_specs=[pl.BlockSpec(memory_space=pltpu.SMEM), vmem, vmem, anywhere, anywhere],
        out_specs=(vmem, vmem),
        scratch_shapes=[
            pltpu.VMEM((quarter, K), f32),
            pltpu.VMEM((quarter, param_scale.shape[1]), f32),
            pltpu.VMEM((param_scale.shape[1], quarter), f32),
            pltpu.VMEM((slots, quarter), f32),
            dma((2,)),
        ],
    )(table, traces.reshape(-1, K, Z), rows.reshape(-1, 1, Z), coefficients, param_scale)

    npatch = lax.axis_size("patch")
    total = pl.pallas_call(
        total_kernel,
        name="total",
        out_shape=jax.ShapeDtypeStruct((1, quarter), f32),
        in_specs=[vmem],
        out_specs=vmem,
        scratch_shapes=[pltpu.VMEM((npatch, 1, quarter), f32), dma((npatch - 1,)), dma((npatch - 1,)), dma],
        compiler_params=pltpu.CompilerParams(collective_id=1, has_side_effects=True),
    )(partial)
    estimate = jnp.sqrt(total[0] + EPS)
    return (basis[None], norms[None], estimate)


def solution(mesh):
    placed = (
        P("grp", "patch", None, None),
        P("grp", "patch", None),
        P("grp", "patch", None),
        P("grp", "patch", None),
        P(),
        P(),
        P(),
        P(),
    )
    return jax.shard_map(
        body,
        mesh=mesh,
        in_specs=placed,
        out_specs=(P("grp", "patch", None, None), P("patch", "grp", None), P("grp")),
        check_vma=False,
    )
```

```python
import jax
import jax.numpy as jnp
from jax import lax
from jax.experimental import pallas as pl
from jax.experimental.pallas import tpu as pltpu
from jax.sharding import PartitionSpec as P

MESH = pl.DeviceIdType.MESH
OMEGA = 0.8
EPS = 1e-06
ROWS = 32
K = 64
Z = 128
HALO = 7
VMEM_LIMIT = 62 * 1024 * 1024


def position(i):
    core = i & 1
    y = (i >> 1) & 3
    z = (i >> 3) & 3
    x = i >> 5
    last = jnp.where(core == 0, z, y)
    first = jnp.where(core == 0, y, z)
    return core * 64 + last * 16 + x * 4 + first


def round_kernel(
    table, f_hbm, s_hbm, r_hbm, v_hbm, coeffs_hbm, scales_hbm,
    basis_hbm, norms, estimate,
    u0, u1, u2, u3, u4, u5, u6,
    fext, cells, small, coef, spread, out, traces, rows,
    coeffs, scales, scales_t, wide, weights, weights2, fw0, bw0, fw1, bw1, parts, inbox,
    local_sem, halo_send, halo_recv, t_send, t_recv, r_send, r_recv, tp_send, tp_recv, rp_send, rp_recv, out_sem,
    s_send, s_recv,
):
    x = lax.axis_index("grp")
    p = lax.axis_index("patch")
    c = p % 2
    y = (p // 2) % 4
    z = p // 8
    a = jnp.where(c == 0, z, y)
    b = jnp.where(c == 0, y, z)
    npatch = 32
    u = (u0, u1, u2, u3, u4, u5, u6)
    line = c * 64 + a * 16
    plane = line + x * 4
    place = plane + b
    right = (p + 1) % npatch
    left = (p + npatch - 1) % npatch
    partner = p + 1 - 2 * c

    def patch_of(last, first):
        return last * (8 - 6 * c) + first * (2 + 6 * c) + c

    firsts = [(x, patch_of(a, (b + d) % 4)) for d in (1, 2, 3)]
    grps = [((x + d) % 4, p) for d in (1, 2, 3)]
    lasts = [(x, patch_of((a + d) % 4, b)) for d in (1, 2, 3)]
    other = (x, partner)

    own_f = pltpu.make_async_copy(f_hbm, fext.at[pl.ds(8, ROWS)], local_sem.at[0])
    own_cells = [
        pltpu.make_async_copy(ref, cells.at[n, pl.ds(8, ROWS)], local_sem.at[1 + n])
        for n, ref in enumerate((s_hbm, r_hbm, v_hbm))
    ]
    own_row = pltpu.make_async_copy(s_hbm.at[pl.ds(ROWS - 1, 1)], rows.at[place], local_sem.at[4])
    quarter = norms.shape[0]
    own_p = [
        pltpu.make_async_copy(coeffs_hbm.at[pl.ds(x * quarter, quarter)], coeffs, local_sem.at[5]),
        pltpu.make_async_copy(scales_hbm.at[pl.ds(x * quarter, quarter)], scales, local_sem.at[6]),
    ]
    for copy in own_cells + [own_f, own_row] + own_p:
        copy.start()

    barrier = pltpu.get_barrier_semaphore()
    peers = [(x, left), (x, right)] + firsts + grps + lasts + [other]
    for peer in peers:
        pl.semaphore_signal(barrier, inc=1, device_id=peer, device_id_type=MESH)
    pl.semaphore_wait(barrier, len(peers))

    def remote(src, dst, ssem, rsem, device):
        return pltpu.make_async_remote_copy(
            src_ref=src, dst_ref=dst, send_sem=ssem, recv_sem=rsem, device_id=device, device_id_type=MESH
        )

    to_left, to_right = [], []
    for n, ref in enumerate((s_hbm, r_hbm, v_hbm)):
        to_left.append(
            remote(ref.at[pl.ds(0, 8)], cells.at[n, pl.ds(8 + ROWS, 8)], halo_send.at[0, n], halo_recv.at[0, n], (x, left))
        )
        to_right.append(
            remote(ref.at[pl.ds(ROWS - 8, 8)], cells.at[n, pl.ds(0, 8)], halo_send.at[1, n], halo_recv.at[1, n], (x, right))
        )
    to_left.append(
        remote(f_hbm.at[pl.ds(0, HALO)], fext.at[pl.ds(8 + ROWS, HALO)], halo_send.at[0, 3], halo_recv.at[0, 3], (x, left))
    )
    to_right.append(
        remote(f_hbm.at[pl.ds(ROWS - HALO, HALO)], fext.at[pl.ds(8 - HALO, HALO)], halo_send.at[1, 3], halo_recv.at[1, 3], (x, right))
    )
    for copy in to_left:
        copy.start()
    for copy in to_right:
        copy.start()

    def stage1(buf, ssem, rsem):
        return [remote(buf.at[place], buf.at[place], ssem.at[0, n], rsem.at[0, n], dev) for n, dev in enumerate(firsts)]

    def stage2(buf, ssem, rsem):
        return [remote(buf.at[pl.ds(plane, 4)], buf.at[pl.ds(plane, 4)], ssem.at[1, n], rsem.at[1, n], dev) for n, dev in enumerate(grps)]

    def stage3(buf, ssem, rsem):
        return [remote(buf.at[pl.ds(line, 16)], buf.at[pl.ds(line, 16)], ssem.at[2, n], rsem.at[2, n], dev) for n, dev in enumerate(lasts)]

    def start(copies):
        for copy in copies:
            copy.start()

    own_row.wait()
    r1 = stage1(rows, r_send, r_recv)
    start(r1)

    lane = lax.broadcasted_iota(jnp.int32, (8, Z), 1)
    sub = lax.broadcasted_iota(jnp.int32, (8, Z), 0)

    def coefficients(e0):
        mid = cells[0, pl.ds(e0, 8), :]
        row = sub + e0
        keep_w = jnp.where((row == 8) & (p == 0), 0.0, 1.0)
        keep_e = jnp.where((row == 7 + ROWS) & (p == npatch - 1), 0.0, 1.0)
        keep_s = jnp.where(lane == 0, 0.0, 1.0)
        keep_n = jnp.where(lane == Z - 1, 0.0, 1.0)
        west = 0.5 * (mid + keep_w * cells[0, pl.ds(e0 - 1, 8), :])
        east = 0.5 * (mid + keep_e * cells[0, pl.ds(e0 + 1, 8), :])
        south = 0.5 * (mid + keep_s * pltpu.roll(mid, 1, 1))
        north = 0.5 * (mid + keep_n * pltpu.roll(mid, Z - 1, 1))
        volume = cells[2, pl.ds(e0, 8), :]
        rest = cells[1, pl.ds(e0, 8), :] + west + east + south + north
        diagonal = rest + volume
        weight = OMEGA / diagonal
        values = (
            1.0 - weight * rest,
            1.0 - weight * (rest + 3.0 * volume),
            weight * west * keep_w,
            weight * east * keep_e,
            weight * south * keep_s,
            weight * north * keep_n,
            weight * (1.0 / 3.0),
        )
        for n, value in enumerate(values):
            small[n] = value
        for n in range(7):
            for k in range(8):
                coef[n, e0 + k] = jnp.broadcast_to(small[n, pl.ds(k, 1), :], (8, Z))

    def first_level(e, slot):
        spread[slot] = fext[e].astype(jnp.float32)
        parts = [spread[slot, pl.ds(n, K, stride=3), :].reshape(8, 8, Z) for n in range(3)]
        weight = coef[6, e][None]
        total = parts[0] + parts[1] + parts[2]
        u0[e, 0:8] = weight * total
        u0[e, 8:16] = weight * (3.0 * parts[0] - total)
        u0[e, 16:24] = weight * (3.0 * parts[1] - total)

    def turned(value, shift):
        return pltpu.roll(value.reshape(K, Z), shift, 1).reshape(8, 8, Z)

    def update(level, e, m, before, now, after):
        centre = coef[1 if m == 0 else 0, e][None]
        return (
            u0[e, pl.ds(8 * m, 8)]
            + centre * now
            + coef[2, e][None] * before
            + coef[3, e][None] * after
            + coef[4, e][None] * turned(now, 1)
            + coef[5, e][None] * turned(now, Z - 1)
        )

    def sweep(level, e0, n):
        for m in range(3):
            part = pl.ds(8 * m, 8)
            before = u[level - 2][e0 - 1, part]
            now = u[level - 2][e0, part]
            for k in range(n):
                after = u[level - 2][e0 + k + 1, part]
                u[level - 1][e0 + k, part] = update(level, e0 + k, m, before, now, after)
                before, now = now, after

    def last_modes(e, count):
        result = []
        for m in range(count):
            part = pl.ds(8 * m, 8)
            result.append(update(8, e, m, u6[e - 1, part], u6[e, part], u6[e + 1, part]))
        return result

    def emit(e, slot):
        total, first, second = last_modes(e, 3)
        values = (total + first, total + second, total - first - second)
        for n, value in enumerate(values):
            spread[slot, pl.ds(n, K, stride=3), :] = value.reshape(K, Z)
        out[e - 8] = spread[slot].astype(jnp.bfloat16)

    for copy in own_cells:
        copy.wait()
    for e0 in (9, 17, 25, 31):
        coefficients(e0)
    own_f.wait()

    def pair_first(i, carry):
        first_level(9 + 2 * i, 0)
        first_level(10 + 2 * i, 1)
        return carry

    lax.fori_loop(0, 15, pair_first, 0)
    def rise(level, e0, n):
        def pair(i, carry):
            sweep(level, e0 + 2 * i, 2)
            return carry

        lax.fori_loop(0, n // 2, pair, 0)

    for level in range(2, 8):
        rise(level, 8 + level, 32 - 2 * level)

    def finish(copies):
        for copy in copies:
            copy.wait_recv()

    finish(r1)
    r2 = stage2(rows, r_send, r_recv)
    start(r2)

    finish(to_left)
    coefficients(39)

    def right_first(i, carry):
        first_level(39 + 2 * i, 0)
        first_level(40 + 2 * i, 1)
        return carry

    lax.fori_loop(0, 4, right_first, 0)

    for level in range(2, 8):
        rise(level, 40 - level, 8)
    total, first = last_modes(7 + ROWS, 2)
    traces[place] = (total + first).reshape(K, Z).astype(jnp.bfloat16)
    finish(r2)
    r3 = stage3(rows, r_send, r_recv)
    start(r3)
    t1 = stage1(traces, t_send, t_recv)
    start(t1)

    finish(to_right)
    coefficients(1)

    def left_first(i, carry):
        first_level(1 + 2 * i, 0)
        first_level(2 + 2 * i, 1)
        return carry

    lax.fori_loop(0, 4, left_first, 0)

    for level in range(2, 8):
        rise(level, level, 8)

    finish(t1)
    t2 = stage2(traces, t_send, t_recv)
    start(t2)
    finish(r3)
    rp = remote(rows.at[pl.ds(c * 64, 64)], rows.at[pl.ds(c * 64, 64)], rp_send, rp_recv, other)
    rp.start()

    def pair_emit(i, carry):
        emit(8 + 2 * i, 0)
        emit(9 + 2 * i, 1)
        return carry

    half = ROWS // 2
    lax.fori_loop(0, half // 2, pair_emit, 0)
    out0 = pltpu.make_async_copy(out.at[pl.ds(0, half)], basis_hbm.at[pl.ds(0, half)], out_sem.at[0])
    out0.start()

    finish(t2)
    t3 = stage3(traces, t_send, t_recv)
    start(t3)

    def slab(k):
        where = pl.ds(c * 64 + (a + 4 - k) % 4 * 16, 16)
        return remote(traces.at[where], traces.at[where], tp_send.at[k], tp_recv.at[k], other)

    tp = [slab(k) for k in range(4)]
    tp[0].start()

    lax.fori_loop(half // 2, half, pair_emit, 0)
    out1 = pltpu.make_async_copy(out.at[pl.ds(half, half)], basis_hbm.at[pl.ds(half, half)], out_sem.at[1])
    out1.start()

    contract = (((1,), (1,)), ((), ()))

    def product(left_side, right_side):
        return lax.dot_general(left_side, right_side, contract, preferred_element_type=jnp.float32)

    for copy in own_p:
        copy.wait()
    scales_t[...] = scales[...].T
    weights[...] = coeffs[...].astype(jnp.bfloat16)
    wide[...] = jnp.zeros_like(wide)
    wide[:, 0:K] = coeffs[...]
    low = wide[...]
    weights2[0:quarter] = low.astype(jnp.bfloat16)
    weights2[quarter : 2 * quarter] = pltpu.roll(low, K, 1).astype(jnp.bfloat16)

    for n in (0, 2, 1):
        t3[n].wait_recv()
        tp[n + 1].start()
    rp.wait_recv()
    finish(tp)

    def pick(slot):
        return jnp.maximum(table[slot], 0)

    def blocks(n, forward, backward):
        for q in range(4):
            i = 4 * n + q
            where = position(i)
            scaled = (traces[where].astype(jnp.float32) * rows[where]).astype(jnp.bfloat16)
            pair = jnp.concatenate([traces[position(pick(2 * i))], traces[position(pick(2 * i + 1))]], axis=0)
            forward[K * q : K * q + K] = product(scaled, pair).astype(jnp.bfloat16)
            backward[2 * K * q : 2 * K * q + 2 * K] = product(pair, scaled).astype(jnp.bfloat16)

    def residuals(n, forward, backward):
        ahead = product(forward[...], weights2[...])
        behind = product(backward[...], weights[...])
        for q in range(4):
            i = 4 * n + q
            own = scales_t[pl.ds(i, 1), :]
            for k in range(2):
                slot = 2 * i + k
                beside = scales_t[pl.ds(pick(slot), 1), :]
                residual = (
                    own * ahead[K * q : K * q + K, quarter * k : quarter * k + quarter]
                    - beside * behind[2 * K * q + K * k : 2 * K * q + K * k + K]
                )
                part = jnp.sum((residual * residual).reshape(8, 8, quarter), axis=0)
                parts[pl.ds(pl.multiple_of(8 * slot, 8), 8), :] = jnp.where(table[slot] >= 0, part, 0.0)

    chunks = traces.shape[0] // 4
    blocks(0, fw0, bw0)

    def two(i, carry):
        blocks(2 * i + 1, fw1, bw1)
        residuals(2 * i, fw0, bw0)
        blocks(jnp.minimum(2 * i + 2, chunks - 1), fw0, bw0)
        residuals(2 * i + 1, fw1, bw1)
        return carry

    lax.fori_loop(0, chunks // 2, two, 0)
    slots = norms.shape[1]
    squares = parts[pl.ds(0, slots, stride=8), :]
    for n in range(1, 8):
        squares = squares + parts[pl.ds(n, slots, stride=8), :]
    inbox[p] = jnp.sum(squares, axis=0, keepdims=True)
    norms[...] = jnp.sqrt(squares.T + EPS)
    shares = [
        remote(inbox.at[p], inbox.at[p], s_send.at[d - 1], s_recv.at[d - 1], (x, (p + d) % npatch))
        for d in range(1, npatch)
    ]
    start(shares)
    finish(shares)
    total = inbox[0]
    for n in range(1, npatch):
        total = total + inbox[n]
    estimate[...] = jnp.sqrt(total + EPS)
    for copy in to_left + to_right + r1 + r2 + r3 + [rp] + t1 + t2 + t3 + tp + shares:
        copy.wait_send()
    for copy in (out0, out1):
        copy.wait()


def owned(owner_map, adjacency, owner):
    mine = owner_map == owner
    earlier = jnp.pad(mine, ((0, 0), (1, 0)))[:, :-1]
    picked = jnp.stack([mine & ~earlier, mine & earlier], axis=1)
    found = jnp.sum(jnp.where(picked, adjacency[:, None, :] + 1, 0), axis=2)
    return (found - 1).reshape(-1)


def body(forcing, stiffness, reaction, volumetric, adjacency, owner_map, param_scale, coefficients):
    anywhere = pl.BlockSpec(memory_space=pl.ANY)
    vmem = pl.BlockSpec(memory_space=pltpu.VMEM)
    dma = pltpu.SemaphoreType.DMA
    f32, bf16 = jnp.float32, jnp.bfloat16
    table = owned(owner_map, adjacency, lax.axis_index("patch"))
    slots = table.shape[0]
    quarter = param_scale.shape[0] // lax.axis_size("grp")
    npatch = lax.axis_size("patch")
    basis, norms, estimate = pl.pallas_call(
        round_kernel,
        name="round",
        out_shape=(
            jax.ShapeDtypeStruct((ROWS, 3 * K, Z), bf16),
            jax.ShapeDtypeStruct((quarter, slots), f32),
            jax.ShapeDtypeStruct((1, quarter), f32),
        ),
        in_specs=[pl.BlockSpec(memory_space=pltpu.SMEM)] + [anywhere] * 6,
        out_specs=(anywhere, vmem, vmem),
        scratch_shapes=[pltpu.VMEM((48, 24, 8, Z), f32)] * 7
        + [
            pltpu.VMEM((48, 3 * K, Z), bf16),
            pltpu.VMEM((3, 48, Z), f32),
            pltpu.VMEM((7, 8, Z), f32),
            pltpu.VMEM((7, 48, 8, Z), f32),
            pltpu.VMEM((2, 3 * K, Z), f32),
            pltpu.VMEM((ROWS, 3 * K, Z), bf16),
            pltpu.VMEM((128, K, Z), bf16),
            pltpu.VMEM((128, 1, Z), f32),
            pltpu.VMEM((quarter, K), f32),
            pltpu.VMEM((quarter, 128), f32),
            pltpu.VMEM((128, quarter), f32),
            pltpu.VMEM((quarter, 2 * K), f32),
            pltpu.VMEM((quarter, K), bf16),
            pltpu.VMEM((2 * quarter, 2 * K), bf16),
            pltpu.VMEM((4 * K, 2 * K), bf16),
            pltpu.VMEM((8 * K, K), bf16),
            pltpu.VMEM((4 * K, 2 * K), bf16),
            pltpu.VMEM((8 * K, K), bf16),
            pltpu.VMEM((8 * slots, quarter), f32),
            pltpu.VMEM((npatch, 1, quarter), f32),
            dma((7,)),
            dma((2, 4)),
            dma((2, 4)),
            dma((3, 3)),
            dma((3, 3)),
            dma((3, 3)),
            dma((3, 3)),
            dma((4,)),
            dma((4,)),
            dma,
            dma,
            dma((2,)),
            dma((npatch - 1,)),
            dma((npatch - 1,)),
        ],
        compiler_params=pltpu.CompilerParams(collective_id=0, has_side_effects=True, vmem_limit_bytes=VMEM_LIMIT),
    )(table, forcing[0], stiffness[0], reaction[0], volumetric[0], coefficients, param_scale)
    return (basis[None], norms[None], estimate[0])


def solution(mesh):
    placed = (
        P("grp", "patch", None, None),
        P("grp", "patch", None),
        P("grp", "patch", None),
        P("grp", "patch", None),
        P(),
        P(),
        P(),
        P(),
    )
    return jax.shard_map(
        body,
        mesh=mesh,
        in_specs=placed,
        out_specs=(P("grp", "patch", None, None), P("patch", "grp", None), P("grp")),
        check_vma=False,
    )
```

```python
import jax
import jax.numpy as jnp
from jax import lax
from jax.experimental import pallas as pl
from jax.experimental.pallas import tpu as pltpu
from jax.sharding import PartitionSpec as P

MESH = pl.DeviceIdType.MESH
OMEGA = 0.8
EPS = 1e-06
ROWS = 32
K = 64
Z = 128
HALO = 7
VMEM_LIMIT = 62 * 1024 * 1024


def position(i):
    core = i & 1
    y = (i >> 1) & 3
    z = (i >> 3) & 3
    x = i >> 5
    last = jnp.where(core == 0, z, y)
    first = jnp.where(core == 0, y, z)
    return core * 64 + last * 16 + x * 4 + first


def round_kernel(
    f_hbm, s_hbm, r_hbm, v_hbm, coeffs_hbm, scales_hbm, owners_hbm, adjacent_hbm,
    basis_hbm, norms, estimate,
    u0, u1, u2, u3, u4, u5, u6,
    fext, cells, small, coef, spread, out, traces, rows,
    owners, adjacent, found, table, shuffle, split, coeffs, scales, scales_t, weights, weights2, fw0, bw0, fw1, bw1, parts, inbox,
    local_sem, halo_send, halo_recv, t_send, t_recv, r_send, r_recv, tp_send, tp_recv, rp_send, rp_recv, out_sem,
    s_send, s_recv,
):
    x = lax.axis_index("grp")
    p = lax.axis_index("patch")
    c = p % 2
    y = (p // 2) % 4
    z = p // 8
    a = jnp.where(c == 0, z, y)
    b = jnp.where(c == 0, y, z)
    npatch = 32
    u = (u0, u1, u2, u3, u4, u5, u6)
    line = c * 64 + a * 16
    plane = line + x * 4
    place = plane + b
    right = (p + 1) % npatch
    left = (p + npatch - 1) % npatch
    partner = p + 1 - 2 * c

    def patch_of(last, first):
        return last * (8 - 6 * c) + first * (2 + 6 * c) + c

    firsts = [(x, patch_of(a, (b + d) % 4)) for d in (1, 2, 3)]
    grps = [((x + d) % 4, p) for d in (1, 2, 3)]
    lasts = [(x, patch_of((a + d) % 4, b)) for d in (1, 2, 3)]
    other = (x, partner)

    own_f = pltpu.make_async_copy(f_hbm, fext.at[pl.ds(8, ROWS)], local_sem.at[0])
    own_cells = [
        pltpu.make_async_copy(ref, cells.at[n, pl.ds(8, ROWS)], local_sem.at[1 + n])
        for n, ref in enumerate((s_hbm, r_hbm, v_hbm))
    ]
    own_row = pltpu.make_async_copy(s_hbm.at[pl.ds(ROWS - 1, 1)], rows.at[place], local_sem.at[4])
    quarter = norms.shape[0]
    own_p = [
        pltpu.make_async_copy(coeffs_hbm.at[:, pl.ds(x * quarter, quarter)], coeffs, local_sem.at[5]),
        pltpu.make_async_copy(scales_hbm.at[pl.ds(x * quarter, quarter)], scales, local_sem.at[6]),
    ]
    own_t = [
        pltpu.make_async_copy(owners_hbm, owners, local_sem.at[7]),
        pltpu.make_async_copy(adjacent_hbm, adjacent, local_sem.at[8]),
    ]
    for copy in own_cells + [own_f, own_row] + own_t + own_p:
        copy.start()

    barrier = pltpu.get_barrier_semaphore()
    peers = [(x, left), (x, right)] + firsts + grps + lasts + [other]
    for peer in peers:
        pl.semaphore_signal(barrier, inc=1, device_id=peer, device_id_type=MESH)

    side = lax.broadcasted_iota(jnp.int32, (2 * Z, 2 * Z), 0)
    lanes = lax.broadcasted_iota(jnp.int32, (2 * Z, 2 * Z), 1)
    cell = 2 * (lanes & 63) + (lanes >> 7)
    same_cell = (side & 127) == cell
    shuffle[...] = jnp.where(same_cell & ((side >> 7) == ((lanes >> 6) & 1)), 1.0, 0.0).astype(jnp.bfloat16)
    split[...] = jnp.where(same_cell[0:Z], 1.0, 0.0)
    for copy in own_t:
        copy.wait()
    found[...] = jnp.zeros_like(found)
    count = jnp.zeros((1, Z), jnp.int32)
    picked = [count, count]
    for n in range(owners.shape[0]):
        mine = jnp.where(owners[pl.ds(n, 1), :] == p, 1, 0)
        entry = adjacent[pl.ds(n, 1), :] + 1
        for k in range(2):
            picked[k] = picked[k] + jnp.where(count == k, mine * entry, 0)
        count = count + mine
    for k in range(2):
        found[pl.ds(k, 1), :] = picked[k] - 1
    pl.semaphore_wait(barrier, len(peers))

    def remote(src, dst, ssem, rsem, device):
        return pltpu.make_async_remote_copy(
            src_ref=src, dst_ref=dst, send_sem=ssem, recv_sem=rsem, device_id=device, device_id_type=MESH
        )

    to_left, to_right = [], []
    for n, ref in enumerate((s_hbm, r_hbm, v_hbm)):
        to_left.append(
            remote(ref.at[pl.ds(0, 8)], cells.at[n, pl.ds(8 + ROWS, 8)], halo_send.at[0, n], halo_recv.at[0, n], (x, left))
        )
        to_right.append(
            remote(ref.at[pl.ds(ROWS - 8, 8)], cells.at[n, pl.ds(0, 8)], halo_send.at[1, n], halo_recv.at[1, n], (x, right))
        )
    to_left.append(
        remote(f_hbm.at[pl.ds(0, HALO)], fext.at[pl.ds(8 + ROWS, HALO)], halo_send.at[0, 3], halo_recv.at[0, 3], (x, left))
    )
    to_right.append(
        remote(f_hbm.at[pl.ds(ROWS - HALO, HALO)], fext.at[pl.ds(8 - HALO, HALO)], halo_send.at[1, 3], halo_recv.at[1, 3], (x, right))
    )
    for copy in to_left:
        copy.start()
    for copy in to_right:
        copy.start()

    def stage1(buf, ssem, rsem):
        return [remote(buf.at[place], buf.at[place], ssem.at[0, n], rsem.at[0, n], dev) for n, dev in enumerate(firsts)]

    def stage2(buf, ssem, rsem):
        return [remote(buf.at[pl.ds(plane, 4)], buf.at[pl.ds(plane, 4)], ssem.at[1, n], rsem.at[1, n], dev) for n, dev in enumerate(grps)]

    def stage3(buf, ssem, rsem):
        return [remote(buf.at[pl.ds(line, 16)], buf.at[pl.ds(line, 16)], ssem.at[2, n], rsem.at[2, n], dev) for n, dev in enumerate(lasts)]

    def start(copies):
        for copy in copies:
            copy.start()

    own_row.wait()
    r1 = stage1(rows, r_send, r_recv)
    start(r1)

    lane = lax.broadcasted_iota(jnp.int32, (8, Z), 1)
    sub = lax.broadcasted_iota(jnp.int32, (8, Z), 0)

    def coefficients(e0):
        mid = cells[0, pl.ds(e0, 8), :]
        row = sub + e0
        keep_w = jnp.where((row == 8) & (p == 0), 0.0, 1.0)
        keep_e = jnp.where((row == 7 + ROWS) & (p == npatch - 1), 0.0, 1.0)
        keep_s = jnp.where(lane == 0, 0.0, 1.0)
        keep_n = jnp.where(lane == Z - 1, 0.0, 1.0)
        west = 0.5 * (mid + keep_w * cells[0, pl.ds(e0 - 1, 8), :])
        east = 0.5 * (mid + keep_e * cells[0, pl.ds(e0 + 1, 8), :])
        south = 0.5 * (mid + keep_s * pltpu.roll(mid, 1, 1))
        north = 0.5 * (mid + keep_n * pltpu.roll(mid, Z - 1, 1))
        volume = cells[2, pl.ds(e0, 8), :]
        rest = cells[1, pl.ds(e0, 8), :] + west + east + south + north
        diagonal = rest + volume
        weight = OMEGA / diagonal
        values = (
            1.0 - weight * rest,
            1.0 - weight * (rest + 3.0 * volume),
            weight * west * keep_w,
            weight * east * keep_e,
            weight * south * keep_s,
            weight * north * keep_n,
            weight * (1.0 / 3.0),
        )
        parted = lax.dot_general(
            jnp.concatenate(values, axis=0), split[...], (((1,), (0,)), ((), ())),
            precision=lax.Precision.HIGHEST, preferred_element_type=jnp.float32,
        )
        small[...] = parted
        for n in range(7):
            for parity in range(2):
                kind = 9 - n if n in (4, 5) and parity == 0 else n
                for k in range(8):
                    row = small[pl.ds(8 * n + k, 1), Z * parity : Z * parity + Z]
                    coef[kind, e0 + k, parity] = jnp.broadcast_to(row, (8, Z))

    half = 3 * K // 2
    plain = (((1,), (0,)), ((), ()))
    contract = (((1,), (1,)), ((), ()))

    def product(left_side, right_side, dims=contract):
        return lax.dot_general(left_side, right_side, dims, preferred_element_type=jnp.float32)

    def block(m, parity):
        return pl.ds(8 * m + 4 * parity, 4)

    def first_level(e, slot):
        value = fext[e]
        parted = product(jnp.concatenate([value[0:half], value[half:]], axis=1), shuffle[...], plain)
        for parity in range(2):
            spread[slot, parity] = parted[:, Z * parity : Z * parity + Z]
        for parity in range(2):
            parts = [spread[slot, parity, pl.ds(n, K // 2, stride=3), :].reshape(4, 8, Z) for n in range(3)]
            weight = coef[6, e, parity][None]
            total = parts[0] + parts[1] + parts[2]
            u0[e, block(0, parity)] = weight * total
            u0[e, block(1, parity)] = weight * (3.0 * parts[0] - total)
            u0[e, block(2, parity)] = weight * (3.0 * parts[1] - total)

    def first_levels(e0, n):
        def four(i, carry):
            for k in range(4):
                first_level(e0 + 4 * i + k, k)
            return carry

        lax.fori_loop(0, n // 4, four, 0)

    def turned(value, shift):
        return pltpu.roll(value.reshape(K // 2, Z), shift, 1).reshape(4, 8, Z)

    def update(e, m, parity, before, now, after, beside):
        centre = coef[1 if m == 0 else 0, e, parity][None]
        return (
            u0[e, block(m, parity)]
            + coef[2, e, parity][None] * before
            + coef[3, e, parity][None] * after
        ) + (
            centre * now
            + (coef[4, e, parity][None] * beside + coef[5, e, parity][None] * turned(beside, 1 if parity == 0 else Z - 1))
        )

    def sweep(level, e0, n):
        below, mine = u[level - 2], u[level - 1]
        for m in range(3):
            for parity in range(2):
                part = block(m, parity)
                before = below[e0 - 1, part]
                now = below[e0, part]
                for k in range(n):
                    after = below[e0 + k + 1, part]
                    beside = below[e0 + k, block(m, 1 - parity)]
                    mine[e0 + k, part] = update(e0 + k, m, parity, before, now, after, beside)
                    before, now = now, after

    def last_modes(e, count):
        result = []
        for m in range(count):
            both = []
            for parity in range(2):
                part = block(m, parity)
                beside = u6[e, block(m, 1 - parity)]
                both.append(update(e, m, parity, u6[e - 1, part], u6[e, part], u6[e + 1, part], beside))
            result.append(both)
        return result

    def emit(e, slot):
        total, first, second = last_modes(e, 3)
        for parity in range(2):
            t, f, g = total[parity], first[parity], second[parity]
            for n, value in enumerate((t + f, t + g, t - f - g)):
                spread[slot, parity, pl.ds(n, K // 2, stride=3), :] = value.reshape(K // 2, Z)
        value = jnp.concatenate([spread[slot, 0], spread[slot, 1]], axis=1).astype(jnp.bfloat16)
        joined = product(value, shuffle[...]).astype(jnp.bfloat16)
        out[e - 8, 0:half] = joined[:, 0:Z]
        out[e - 8, half:] = joined[:, Z:]

    for copy in own_cells:
        copy.wait()
    for e0 in (9, 17, 25, 31):
        coefficients(e0)
    own_f.wait()

    first_levels(8, ROWS)
    for level in range(2, 8):
        eights, fours = divmod((32 - 2 * level + 3) // 4, 2)

        def eight(i, carry, level=level):
            sweep(level, 8 + level + 8 * i, 8)
            return carry

        lax.fori_loop(0, eights, eight, 0)
        if fours:
            sweep(level, 8 + level + 8 * eights, 4)

    def finish(copies):
        for copy in copies:
            copy.wait_recv()

    finish(r1)
    r2 = stage2(rows, r_send, r_recv)
    start(r2)

    finish(to_left)
    coefficients(39)

    first_levels(39, 8)
    for level in range(2, 8):
        sweep(level, 40 - level, 8)
    total, first = last_modes(7 + ROWS, 2)
    ends = [(total[parity] + first[parity]).reshape(K // 2, Z).astype(jnp.bfloat16) for parity in range(2)]
    trace = product(jnp.concatenate(ends, axis=1), shuffle[...]).astype(jnp.bfloat16)
    traces[place, 0 : K // 2] = trace[:, 0:Z]
    traces[place, K // 2 :] = trace[:, Z:]
    finish(r2)
    r3 = stage3(rows, r_send, r_recv)
    start(r3)
    t1 = stage1(traces, t_send, t_recv)
    start(t1)

    finish(to_right)
    coefficients(1)

    first_levels(1, 8)
    for level in range(2, 8):
        sweep(level, level, 8)

    finish(t1)
    t2 = stage2(traces, t_send, t_recv)
    start(t2)
    finish(r3)
    rp = remote(rows.at[pl.ds(c * 64, 64)], rows.at[pl.ds(c * 64, 64)], rp_send, rp_recv, other)
    rp.start()

    def four_emit(i, carry):
        for k in range(4):
            emit(8 + 4 * i + k, k)
        return carry

    middle = ROWS // 2
    lax.fori_loop(0, middle // 4, four_emit, 0)
    out0 = pltpu.make_async_copy(out.at[pl.ds(0, middle)], basis_hbm.at[pl.ds(0, middle)], out_sem.at[0])
    out0.start()

    finish(t2)
    t3 = stage3(traces, t_send, t_recv)
    start(t3)

    def slab(k):
        where = pl.ds(c * 64 + (a + 4 - k) % 4 * 16, 16)
        return remote(traces.at[where], traces.at[where], tp_send.at[k], tp_recv.at[k], other)

    tp = [slab(k) for k in range(4)]
    tp[0].start()

    lax.fori_loop(middle // 4, ROWS // 4, four_emit, 0)
    out1 = pltpu.make_async_copy(out.at[pl.ds(middle, middle)], basis_hbm.at[pl.ds(middle, middle)], out_sem.at[1])
    out1.start()

    to_table = pltpu.make_async_copy(found, table, local_sem.at[9])
    to_table.start()
    for copy in own_p:
        copy.wait()
    scales_t[...] = scales[...].T
    narrow = coeffs[...].astype(jnp.bfloat16)
    weights[...] = narrow
    weights2[...] = jnp.zeros_like(weights2)
    weights2[0:K, 0:quarter] = narrow
    weights2[K:, quarter:] = narrow
    to_table.wait()

    for n in (0, 2, 1):
        t3[n].wait_recv()
        tp[n + 1].start()
    rp.wait_recv()
    finish(tp)

    def pick(i, k):
        return jnp.maximum(table[k, i], 0)

    def blocks(n, forward, backward):
        for q in range(4):
            i = 4 * n + q
            where = position(i)
            scaled = (traces[where].astype(jnp.float32) * rows[where]).astype(jnp.bfloat16)
            pair = jnp.concatenate([traces[position(pick(i, 0))], traces[position(pick(i, 1))]], axis=0)
            forward[K * q : K * q + K] = product(scaled, pair).astype(jnp.bfloat16)
            backward[2 * K * q : 2 * K * q + 2 * K] = product(pair, scaled).astype(jnp.bfloat16)

    def residuals(n, forward, backward):
        ahead = product(forward[...], weights2[...], plain)
        behind = product(backward[...], weights[...], plain)
        for q in range(4):
            i = 4 * n + q
            own = scales_t[pl.ds(i, 1), :]
            for k in range(2):
                slot = 2 * i + k
                beside = scales_t[pl.ds(pick(i, k), 1), :]
                residual = (
                    own * ahead[K * q : K * q + K, quarter * k : quarter * k + quarter]
                    - beside * behind[2 * K * q + K * k : 2 * K * q + K * k + K]
                )
                part = jnp.sum((residual * residual).reshape(8, 8, quarter), axis=0)
                parts[pl.ds(pl.multiple_of(8 * slot, 8), 8), :] = jnp.where(table[k, i] >= 0, part, 0.0)

    chunks = traces.shape[0] // 4
    blocks(0, fw0, bw0)

    def two(i, carry):
        blocks(2 * i + 1, fw1, bw1)
        residuals(2 * i, fw0, bw0)
        blocks(jnp.minimum(2 * i + 2, chunks - 1), fw0, bw0)
        residuals(2 * i + 1, fw1, bw1)
        return carry

    lax.fori_loop(0, chunks // 2, two, 0)
    slots = norms.shape[1]
    squares = parts[pl.ds(0, slots, stride=8), :]
    for n in range(1, 8):
        squares = squares + parts[pl.ds(n, slots, stride=8), :]
    inbox[p] = jnp.sum(squares, axis=0, keepdims=True)
    norms[...] = jnp.sqrt(squares.T + EPS)
    shares = [
        remote(inbox.at[p], inbox.at[p], s_send.at[d - 1], s_recv.at[d - 1], (x, (p + d) % npatch))
        for d in range(1, npatch)
    ]
    start(shares)
    finish(shares)
    total = inbox[0]
    for n in range(1, npatch):
        total = total + inbox[n]
    estimate[...] = jnp.sqrt(total + EPS)
    for copy in to_left + to_right + r1 + r2 + r3 + [rp] + t1 + t2 + t3 + tp + shares:
        copy.wait_send()
    for copy in (out0, out1):
        copy.wait()


def body(forcing, stiffness, reaction, volumetric, adjacency, owner_map, param_scale, coefficients):
    anywhere = pl.BlockSpec(memory_space=pl.ANY)
    vmem = pl.BlockSpec(memory_space=pltpu.VMEM)
    dma = pltpu.SemaphoreType.DMA
    f32, bf16 = jnp.float32, jnp.bfloat16
    slots = 2 * owner_map.shape[0]
    quarter = param_scale.shape[0] // lax.axis_size("grp")
    npatch = lax.axis_size("patch")
    basis, norms, estimate = pl.pallas_call(
        round_kernel,
        name="round",
        out_shape=(
            jax.ShapeDtypeStruct((ROWS, 3 * K, Z), bf16),
            jax.ShapeDtypeStruct((quarter, slots), f32),
            jax.ShapeDtypeStruct((1, quarter), f32),
        ),
        in_specs=[anywhere] * 8,
        out_specs=(anywhere, vmem, vmem),
        scratch_shapes=[pltpu.VMEM((48, 24, 8, Z), f32)] * 7
        + [
            pltpu.VMEM((48, 3 * K, Z), bf16),
            pltpu.VMEM((3, 48, Z), f32),
            pltpu.VMEM((56, 2 * Z), f32),
            pltpu.VMEM((7, 48, 2, 8, Z), f32),
            pltpu.VMEM((4, 2, 3 * K // 2, Z), f32),
            pltpu.VMEM((ROWS, 3 * K, Z), bf16),
            pltpu.VMEM((128, K, Z), bf16),
            pltpu.VMEM((128, 1, Z), f32),
            pltpu.VMEM(owner_map.T.shape, jnp.int32),
            pltpu.VMEM(owner_map.T.shape, jnp.int32),
            pltpu.VMEM((8, Z), jnp.int32),
            pltpu.SMEM((8, Z), jnp.int32),
            pltpu.VMEM((2 * Z, 2 * Z), bf16),
            pltpu.VMEM((Z, 2 * Z), f32),
            pltpu.VMEM((K, quarter), f32),
            pltpu.VMEM((quarter, 128), f32),
            pltpu.VMEM((128, quarter), f32),
            pltpu.VMEM((K, quarter), bf16),
            pltpu.VMEM((2 * K, 2 * quarter), bf16),
            pltpu.VMEM((4 * K, 2 * K), bf16),
            pltpu.VMEM((8 * K, K), bf16),
            pltpu.VMEM((4 * K, 2 * K), bf16),
            pltpu.VMEM((8 * K, K), bf16),
            pltpu.VMEM((8 * slots, quarter), f32),
            pltpu.VMEM((npatch, 1, quarter), f32),
            dma((10,)),
            dma((2, 4)),
            dma((2, 4)),
            dma((3, 3)),
            dma((3, 3)),
            dma((3, 3)),
            dma((3, 3)),
            dma((4,)),
            dma((4,)),
            dma,
            dma,
            dma((2,)),
            dma((npatch - 1,)),
            dma((npatch - 1,)),
        ],
        compiler_params=pltpu.CompilerParams(collective_id=0, has_side_effects=True, vmem_limit_bytes=VMEM_LIMIT),
    )(
        forcing[0], stiffness[0], reaction[0], volumetric[0], coefficients.T, param_scale, owner_map.T, adjacency.T
    )
    return (basis[None], norms[None], estimate[0])


def solution(mesh):
    placed = (
        P("grp", "patch", None, None),
        P("grp", "patch", None),
        P("grp", "patch", None),
        P("grp", "patch", None),
        P(),
        P(),
        P(),
        P(),
    )
    return jax.shard_map(
        body,
        mesh=mesh,
        in_specs=placed,
        out_specs=(P("grp", "patch", None, None), P("patch", "grp", None), P("grp")),
        check_vma=False,
    )
```

```python
import jax
import jax.numpy as jnp
from jax import lax
from jax.experimental import pallas as pl
from jax.experimental.pallas import tpu as pltpu
from jax.sharding import PartitionSpec as P

MESH = pl.DeviceIdType.MESH
OMEGA = 0.8
EPS = 1e-06
ROWS = 32
K = 64
Z = 128
HALO = 7
VMEM_LIMIT = 62 * 1024 * 1024


def position(i):
    core = i & 1
    y = (i >> 1) & 3
    z = (i >> 3) & 3
    x = i >> 5
    return core * 64 + jnp.where(core == 0, z * 16 + x * 4 + y, x * 16 + y * 4 + z)


def round_kernel(
    f_hbm, s_hbm, r_hbm, v_hbm, coeffs_hbm, scales_hbm, owners_hbm, adjacent_hbm,
    basis_hbm, norms, estimate,
    u0, u1, u2, u3, u4, u5, u6,
    fext, cells, small, coef, spread, out, traces, rows,
    owners, adjacent, found, table, shuffle, split, coeffs, scales, scales_t, weights, weights2, fw0, bw0, fw1, bw1, parts, inbox,
    local_sem, halo_send, halo_recv, t_send, t_recv, r_send, r_recv, f_send, f_recv, tp_send, tp_recv, rp_send, rp_recv, out_sem,
    s_send, s_recv,
):
    x = lax.axis_index("grp")
    p = lax.axis_index("patch")
    c = p % 2
    y = (p // 2) % 4
    z = p // 8
    a = jnp.where(c == 0, z, x)
    m = jnp.where(c == 0, x, y)
    b = jnp.where(c == 0, y, z)
    npatch = 32
    u = (u0, u1, u2, u3, u4, u5, u6)
    line = c * 64 + a * 16
    plane = line + m * 4
    place = plane + b
    right = (p + 1) % npatch
    left = (p + npatch - 1) % npatch
    partner = p + 1 - 2 * c

    def device(last, middle, first):
        last, middle, first = last % 4, middle % 4, first % 4
        far = jnp.where(c == 0, last, first) * 8 + jnp.where(c == 0, first, middle) * 2 + c
        return (jnp.where(c == 0, middle, last), far)

    firsts = [device(a, m, b + d) for d in (1, 2, 3)]
    grps = [device(a, m + d, b) for d in (1, 2, 3)]
    lasts = [device(a + d, m, b) for d in (1, 2, 3)]
    other = (x, partner)

    own_f = pltpu.make_async_copy(f_hbm, fext.at[pl.ds(8, ROWS)], local_sem.at[0])
    own_cells = [
        pltpu.make_async_copy(ref, cells.at[n, pl.ds(8, ROWS)], local_sem.at[1 + n])
        for n, ref in enumerate((s_hbm, r_hbm, v_hbm))
    ]
    own_row = pltpu.make_async_copy(s_hbm.at[pl.ds(ROWS - 1, 1)], rows.at[place], local_sem.at[4])
    quarter = norms.shape[0]
    own_p = [
        pltpu.make_async_copy(coeffs_hbm.at[:, pl.ds(x * quarter, quarter)], coeffs, local_sem.at[5]),
        pltpu.make_async_copy(scales_hbm.at[pl.ds(x * quarter, quarter)], scales, local_sem.at[6]),
    ]
    own_t = [
        pltpu.make_async_copy(owners_hbm, owners, local_sem.at[7]),
        pltpu.make_async_copy(adjacent_hbm, adjacent, local_sem.at[8]),
    ]
    for copy in own_cells + [own_f, own_row] + own_t + own_p:
        copy.start()

    barrier = pltpu.get_barrier_semaphore()
    peers = [(x, left), (x, right)] + firsts + grps + lasts + [other]
    for peer in peers:
        pl.semaphore_signal(barrier, inc=1, device_id=peer, device_id_type=MESH)

    side = lax.broadcasted_iota(jnp.int32, (2 * Z, 2 * Z), 0)
    lanes = lax.broadcasted_iota(jnp.int32, (2 * Z, 2 * Z), 1)
    cell = 2 * (lanes & 63) + (lanes >> 7)
    same_cell = (side & 127) == cell
    shuffle[...] = jnp.where(same_cell & ((side >> 7) == ((lanes >> 6) & 1)), 1.0, 0.0).astype(jnp.bfloat16)
    split[...] = jnp.where(same_cell[0:Z], 1.0, 0.0)
    for copy in own_t:
        copy.wait()
    found[...] = jnp.zeros_like(found)
    count = jnp.zeros((1, Z), jnp.int32)
    picked = [count, count]
    for n in range(owners.shape[0]):
        mine = jnp.where(owners[pl.ds(n, 1), :] == p, 1, 0)
        entry = adjacent[pl.ds(n, 1), :] + 1
        for k in range(2):
            picked[k] = picked[k] + jnp.where(count == k, mine * entry, 0)
        count = count + mine
    for k in range(2):
        found[pl.ds(k, 1), :] = picked[k] - 1
    pl.semaphore_wait(barrier, len(peers))

    def remote(src, dst, ssem, rsem, device):
        return pltpu.make_async_remote_copy(
            src_ref=src, dst_ref=dst, send_sem=ssem, recv_sem=rsem, device_id=device, device_id_type=MESH
        )

    to_left, to_right = [], []
    for n, ref in enumerate((s_hbm, r_hbm, v_hbm)):
        to_left.append(
            remote(ref.at[pl.ds(0, 8)], cells.at[n, pl.ds(8 + ROWS, 8)], halo_send.at[0, n], halo_recv.at[0, n], (x, left))
        )
        to_right.append(
            remote(ref.at[pl.ds(ROWS - 8, 8)], cells.at[n, pl.ds(0, 8)], halo_send.at[1, n], halo_recv.at[1, n], (x, right))
        )
    to_left.append(
        remote(f_hbm.at[pl.ds(0, HALO)], fext.at[pl.ds(8 + ROWS, HALO)], halo_send.at[0, 3], halo_recv.at[0, 3], (x, left))
    )
    to_right.append(
        remote(f_hbm.at[pl.ds(ROWS - HALO, HALO)], fext.at[pl.ds(8 - HALO, HALO)], halo_send.at[1, 3], halo_recv.at[1, 3], (x, right))
    )
    for copy in to_left:
        copy.start()
    for copy in to_right:
        copy.start()

    def stage1(buf, ssem, rsem):
        return [remote(buf.at[place], buf.at[place], ssem.at[0, n], rsem.at[0, n], dev) for n, dev in enumerate(firsts)]

    def stage2(buf, ssem, rsem):
        return [remote(buf.at[pl.ds(plane, 4)], buf.at[pl.ds(plane, 4)], ssem.at[1, n], rsem.at[1, n], dev) for n, dev in enumerate(grps)]

    def stage3(buf, ssem, rsem):
        return [remote(buf.at[pl.ds(line, 16)], buf.at[pl.ds(line, 16)], ssem.at[2, n], rsem.at[2, n], dev) for n, dev in enumerate(lasts)]

    def start(copies):
        for copy in copies:
            copy.start()

    own_row.wait()
    r1 = stage1(rows, r_send, r_recv)
    start(r1)

    lane = lax.broadcasted_iota(jnp.int32, (8, Z), 1)
    sub = lax.broadcasted_iota(jnp.int32, (8, Z), 0)

    def coefficients(e0):
        mid = cells[0, pl.ds(e0, 8), :]
        row = sub + e0
        keep_w = jnp.where((row == 8) & (p == 0), 0.0, 1.0)
        keep_e = jnp.where((row == 7 + ROWS) & (p == npatch - 1), 0.0, 1.0)
        keep_s = jnp.where(lane == 0, 0.0, 1.0)
        keep_n = jnp.where(lane == Z - 1, 0.0, 1.0)
        west = 0.5 * (mid + keep_w * cells[0, pl.ds(e0 - 1, 8), :])
        east = 0.5 * (mid + keep_e * cells[0, pl.ds(e0 + 1, 8), :])
        south = 0.5 * (mid + keep_s * pltpu.roll(mid, 1, 1))
        north = 0.5 * (mid + keep_n * pltpu.roll(mid, Z - 1, 1))
        volume = cells[2, pl.ds(e0, 8), :]
        rest = cells[1, pl.ds(e0, 8), :] + west + east + south + north
        diagonal = rest + volume
        weight = OMEGA / diagonal
        values = (
            1.0 - weight * rest,
            1.0 - weight * (rest + 3.0 * volume),
            weight * west * keep_w,
            weight * east * keep_e,
            weight * south * keep_s,
            weight * north * keep_n,
            weight * (1.0 / 3.0),
        )
        parted = lax.dot_general(
            jnp.concatenate(values, axis=0), split[...], (((1,), (0,)), ((), ())),
            precision=lax.Precision.HIGHEST, preferred_element_type=jnp.float32,
        )
        small[...] = parted
        for n in range(7):
            for parity in range(2):
                kind = 9 - n if n in (4, 5) and parity == 0 else n
                for k in range(8):
                    row = small[pl.ds(8 * n + k, 1), Z * parity : Z * parity + Z]
                    coef[kind, e0 + k, parity] = jnp.broadcast_to(row, (8, Z))

    half = 3 * K // 2
    plain = (((1,), (0,)), ((), ()))
    contract = (((1,), (1,)), ((), ()))

    def product(left_side, right_side, dims=contract):
        return lax.dot_general(left_side, right_side, dims, preferred_element_type=jnp.float32)

    def block(m, parity):
        return pl.ds(8 * m + 4 * parity, 4)

    def first_level(e, slot):
        value = fext[e]
        parted = product(jnp.concatenate([value[0:half], value[half:]], axis=1), shuffle[...], plain)
        for parity in range(2):
            spread[slot, parity] = parted[:, Z * parity : Z * parity + Z]
        for parity in range(2):
            parts = [spread[slot, parity, pl.ds(n, K // 2, stride=3), :].reshape(4, 8, Z) for n in range(3)]
            weight = coef[6, e, parity][None]
            total = parts[0] + parts[1] + parts[2]
            u0[e, block(0, parity)] = weight * total
            u0[e, block(1, parity)] = weight * (3.0 * parts[0] - total)
            u0[e, block(2, parity)] = weight * (3.0 * parts[1] - total)

    def first_levels(e0, n):
        def four(i, carry):
            for k in range(4):
                first_level(e0 + 4 * i + k, k)
            return carry

        lax.fori_loop(0, n // 4, four, 0)

    def turned(value, shift):
        return pltpu.roll(value.reshape(K // 2, Z), shift, 1).reshape(4, 8, Z)

    def update(e, m, parity, before, now, after, beside):
        centre = coef[1 if m == 0 else 0, e, parity][None]
        return (
            u0[e, block(m, parity)]
            + coef[2, e, parity][None] * before
            + coef[3, e, parity][None] * after
        ) + (
            centre * now
            + (coef[4, e, parity][None] * beside + coef[5, e, parity][None] * turned(beside, 1 if parity == 0 else Z - 1))
        )

    def sweep(level, e0, n):
        below, mine = u[level - 2], u[level - 1]
        for m in range(3):
            for parity in range(2):
                part = block(m, parity)
                before = below[e0 - 1, part]
                now = below[e0, part]
                for k in range(n):
                    after = below[e0 + k + 1, part]
                    beside = below[e0 + k, block(m, 1 - parity)]
                    mine[e0 + k, part] = update(e0 + k, m, parity, before, now, after, beside)
                    before, now = now, after

    def last_modes(e, count):
        result = []
        for m in range(count):
            both = []
            for parity in range(2):
                part = block(m, parity)
                beside = u6[e, block(m, 1 - parity)]
                both.append(update(e, m, parity, u6[e - 1, part], u6[e, part], u6[e + 1, part], beside))
            result.append(both)
        return result

    def emit(e, slot):
        total, first, second = last_modes(e, 3)
        for parity in range(2):
            t, f, g = total[parity], first[parity], second[parity]
            for n, value in enumerate((t + f, t + g, t - f - g)):
                spread[slot, parity, pl.ds(n, K // 2, stride=3), :] = value.reshape(K // 2, Z)
        value = jnp.concatenate([spread[slot, 0], spread[slot, 1]], axis=1).astype(jnp.bfloat16)
        joined = product(value, shuffle[...]).astype(jnp.bfloat16)
        out[e - 8, 0:half] = joined[:, 0:Z]
        out[e - 8, half:] = joined[:, Z:]

    for copy in own_cells:
        copy.wait()
    for e0 in (9, 17, 25, 31):
        coefficients(e0)
    own_f.wait()

    first_levels(8, ROWS)
    for level in range(2, 8):
        eights, fours = divmod((32 - 2 * level + 3) // 4, 2)

        def eight(i, carry, level=level):
            sweep(level, 8 + level + 8 * i, 8)
            return carry

        lax.fori_loop(0, eights, eight, 0)
        if fours:
            sweep(level, 8 + level + 8 * eights, 4)

    def finish(copies):
        for copy in copies:
            copy.wait_recv()

    finish(r1)
    r2 = stage2(rows, r_send, r_recv)
    start(r2)

    finish(to_left)
    coefficients(39)

    first_levels(39, 8)
    for level in range(2, 8):
        sweep(level, 40 - level, 8)
    total, first = last_modes(7 + ROWS, 2)
    ends = [(total[parity] + first[parity]).reshape(K // 2, Z).astype(jnp.bfloat16) for parity in range(2)]
    trace = product(jnp.concatenate(ends, axis=1), shuffle[...]).astype(jnp.bfloat16)
    traces[place, 0 : K // 2] = trace[:, 0:Z]
    traces[place, K // 2 :] = trace[:, Z:]
    finish(r2)
    r3 = stage3(rows, r_send, r_recv)
    start(r3)
    t1 = stage1(traces, t_send, t_recv)
    start(t1)

    finish(to_right)
    coefficients(1)

    first_levels(1, 8)
    for level in range(2, 8):
        sweep(level, level, 8)

    finish(t1)
    t2 = stage2(traces, t_send, t_recv)
    start(t2)

    def part(back, k):
        return traces.at[pl.ds(c * 64 + (a + 4 - back) % 4 * 16 + (m + k) % 4 * 4, 4)]

    def share(back, k):
        return remote(part(back, k), part(back, k), tp_send.at[back, k], tp_recv.at[back, k], other)

    ahead_of = [remote(part(0, k), part(0, k), f_send.at[0, k], f_recv.at[0, k], lasts[0]) for k in range(4)]
    behind_of = [remote(part(0, k), part(0, k), f_send.at[1, k], f_recv.at[1, k], lasts[2]) for k in range(4)]
    relay = [
        remote(part(1, k), part(1, k), f_send.at[2, k], f_recv.at[2, k], lasts[0])
        if k % 2 == 0
        else remote(part(3, k), part(3, k), f_send.at[2, k], f_recv.at[2, k], lasts[2])
        for k in range(4)
    ]
    tp = [[share(back, k) for k in range(4)] for back in range(4)]

    def spread_out(k):
        ahead_of[k].start()
        behind_of[k].start()
        tp[0][k].start()

    def pass_on(k):
        ahead_of[k].wait_recv()
        if k % 2 == 0:
            relay[k].start()
        behind_of[k].wait_recv()
        if k % 2 == 1:
            relay[k].start()
        tp[1][k].start()
        tp[3][k].start()

    spread_out(0)
    finish(r3)
    rp = remote(rows.at[pl.ds(c * 64, 64)], rows.at[pl.ds(c * 64, 64)], rp_send, rp_recv, other)
    rp.start()

    def four_emit(i, carry):
        for k in range(4):
            emit(8 + 4 * i + k, k)
        return carry

    quarters = []

    def emit_quarter(n):
        lax.fori_loop(2 * n, 2 * n + 2, four_emit, 0)
        rows_out = pl.ds(8 * n, 8)
        copy = pltpu.make_async_copy(out.at[rows_out], basis_hbm.at[rows_out], out_sem.at[n])
        copy.start()
        quarters.append(copy)

    emit_quarter(0)
    emit_quarter(1)
    for k in (1, 3):
        t2[3 - k].wait_recv()
        spread_out(k)
    pass_on(0)
    t2[1].wait_recv()
    spread_out(2)
    emit_quarter(2)
    pass_on(1)
    pass_on(3)
    emit_quarter(3)
    pass_on(2)

    to_table = pltpu.make_async_copy(found, table, local_sem.at[9])
    to_table.start()
    for copy in own_p:
        copy.wait()
    scales_t[...] = scales[...].T
    narrow = coeffs[...].astype(jnp.bfloat16)
    weights[...] = narrow
    weights2[...] = jnp.zeros_like(weights2)
    weights2[0:K, 0:quarter] = narrow
    weights2[K:, quarter:] = narrow
    to_table.wait()

    for k in (0, 1, 3, 2):
        relay[k].wait_recv()
        tp[2][k].start()
    rp.wait_recv()
    for copies in tp:
        finish(copies)

    def pick(i, k):
        return jnp.maximum(table[k, i], 0)

    def blocks(n, forward, backward):
        for q in range(4):
            i = 4 * n + q
            where = position(i)
            scaled = (traces[where].astype(jnp.float32) * rows[where]).astype(jnp.bfloat16)
            pair = jnp.concatenate([traces[position(pick(i, 0))], traces[position(pick(i, 1))]], axis=0)
            forward[K * q : K * q + K] = product(scaled, pair).astype(jnp.bfloat16)
            backward[2 * K * q : 2 * K * q + 2 * K] = product(pair, scaled).astype(jnp.bfloat16)

    def residuals(n, forward, backward):
        ahead = product(forward[...], weights2[...], plain)
        behind = product(backward[...], weights[...], plain)
        for q in range(4):
            i = 4 * n + q
            own = scales_t[pl.ds(i, 1), :]
            for k in range(2):
                slot = 2 * i + k
                beside = scales_t[pl.ds(pick(i, k), 1), :]
                residual = (
                    own * ahead[K * q : K * q + K, quarter * k : quarter * k + quarter]
                    - beside * behind[2 * K * q + K * k : 2 * K * q + K * k + K]
                )
                part = jnp.sum((residual * residual).reshape(8, 8, quarter), axis=0)
                parts[pl.ds(pl.multiple_of(8 * slot, 8), 8), :] = jnp.where(table[k, i] >= 0, part, 0.0)

    chunks = traces.shape[0] // 4
    blocks(0, fw0, bw0)

    def two(i, carry):
        blocks(2 * i + 1, fw1, bw1)
        residuals(2 * i, fw0, bw0)
        blocks(jnp.minimum(2 * i + 2, chunks - 1), fw0, bw0)
        residuals(2 * i + 1, fw1, bw1)
        return carry

    lax.fori_loop(0, chunks // 2, two, 0)
    slots = norms.shape[1]
    squares = parts[pl.ds(0, slots, stride=8), :]
    for n in range(1, 8):
        squares = squares + parts[pl.ds(n, slots, stride=8), :]
    inbox[p] = jnp.sum(squares, axis=0, keepdims=True)
    norms[...] = jnp.sqrt(squares.T + EPS)
    shares = [
        remote(inbox.at[p], inbox.at[p], s_send.at[d - 1], s_recv.at[d - 1], (x, (p + d) % npatch))
        for d in range(1, npatch)
    ]
    start(shares)
    finish(shares)
    total = inbox[0]
    for n in range(1, npatch):
        total = total + inbox[n]
    estimate[...] = jnp.sqrt(total + EPS)
    for copy in to_left + to_right + r1 + r2 + r3 + [rp] + t1 + t2 + ahead_of + behind_of + relay + sum(tp, []) + shares:
        copy.wait_send()
    for copy in quarters:
        copy.wait()


def body(forcing, stiffness, reaction, volumetric, adjacency, owner_map, param_scale, coefficients):
    anywhere = pl.BlockSpec(memory_space=pl.ANY)
    vmem = pl.BlockSpec(memory_space=pltpu.VMEM)
    dma = pltpu.SemaphoreType.DMA
    f32, bf16 = jnp.float32, jnp.bfloat16
    slots = 2 * owner_map.shape[0]
    quarter = param_scale.shape[0] // lax.axis_size("grp")
    npatch = lax.axis_size("patch")
    basis, norms, estimate = pl.pallas_call(
        round_kernel,
        name="round",
        out_shape=(
            jax.ShapeDtypeStruct((ROWS, 3 * K, Z), bf16),
            jax.ShapeDtypeStruct((quarter, slots), f32),
            jax.ShapeDtypeStruct((1, quarter), f32),
        ),
        in_specs=[anywhere] * 8,
        out_specs=(anywhere, vmem, vmem),
        scratch_shapes=[pltpu.VMEM((48, 24, 8, Z), f32)] * 7
        + [
            pltpu.VMEM((48, 3 * K, Z), bf16),
            pltpu.VMEM((3, 48, Z), f32),
            pltpu.VMEM((56, 2 * Z), f32),
            pltpu.VMEM((7, 48, 2, 8, Z), f32),
            pltpu.VMEM((4, 2, 3 * K // 2, Z), f32),
            pltpu.VMEM((ROWS, 3 * K, Z), bf16),
            pltpu.VMEM((128, K, Z), bf16),
            pltpu.VMEM((128, 1, Z), f32),
            pltpu.VMEM(owner_map.T.shape, jnp.int32),
            pltpu.VMEM(owner_map.T.shape, jnp.int32),
            pltpu.VMEM((8, Z), jnp.int32),
            pltpu.SMEM((8, Z), jnp.int32),
            pltpu.VMEM((2 * Z, 2 * Z), bf16),
            pltpu.VMEM((Z, 2 * Z), f32),
            pltpu.VMEM((K, quarter), f32),
            pltpu.VMEM((quarter, 128), f32),
            pltpu.VMEM((128, quarter), f32),
            pltpu.VMEM((K, quarter), bf16),
            pltpu.VMEM((2 * K, 2 * quarter), bf16),
            pltpu.VMEM((4 * K, 2 * K), bf16),
            pltpu.VMEM((8 * K, K), bf16),
            pltpu.VMEM((4 * K, 2 * K), bf16),
            pltpu.VMEM((8 * K, K), bf16),
            pltpu.VMEM((8 * slots, quarter), f32),
            pltpu.VMEM((npatch, 1, quarter), f32),
            dma((10,)),
            dma((2, 4)),
            dma((2, 4)),
            dma((3, 3)),
            dma((3, 3)),
            dma((3, 3)),
            dma((3, 3)),
            dma((3, 4)),
            dma((3, 4)),
            dma((4, 4)),
            dma((4, 4)),
            dma,
            dma,
            dma((4,)),
            dma((npatch - 1,)),
            dma((npatch - 1,)),
        ],
        compiler_params=pltpu.CompilerParams(collective_id=0, has_side_effects=True, vmem_limit_bytes=VMEM_LIMIT),
    )(
        forcing[0], stiffness[0], reaction[0], volumetric[0], coefficients.T, param_scale, owner_map.T, adjacency.T
    )
    return (basis[None], norms[None], estimate[0])


def solution(mesh):
    placed = (
        P("grp", "patch", None, None),
        P("grp", "patch", None),
        P("grp", "patch", None),
        P("grp", "patch", None),
        P(),
        P(),
        P(),
        P(),
    )
    return jax.shard_map(
        body,
        mesh=mesh,
        in_specs=placed,
        out_specs=(P("grp", "patch", None, None), P("patch", "grp", None), P("grp")),
        check_vma=False,
    )
```

```python
import jax
import jax.numpy as jnp
from jax import lax
from jax.experimental import pallas as pl
from jax.experimental.pallas import tpu as pltpu
from jax.sharding import PartitionSpec as P

MESH = pl.DeviceIdType.MESH
OMEGA = 0.8
EPS = 1e-06
ROWS = 32
K = 64
Z = 128
HALO = 7
VMEM_LIMIT = 62 * 1024 * 1024


def position(i):
    core = i & 1
    y = (i >> 1) & 3
    z = (i >> 3) & 3
    x = i >> 5
    return core * 64 + jnp.where(core == 0, z * 16 + x * 4 + y, x * 16 + y * 4 + z)


def round_kernel(
    f_hbm, s_hbm, r_hbm, v_hbm, coeffs_hbm, scales_hbm, owners_hbm, adjacent_hbm,
    basis_hbm, norms, estimate,
    u0, u1, u2, u3, u4, u5, u6,
    fext, cells, small, coef, spread, out, traces, rows,
    owners, adjacent, found, table, shuffle, split, coeffs, scales, scales_t, weights, weights2, fw0, bw0, fw1, bw1, parts, inbox,
    local_sem, halo_send, halo_recv, t_send, t_recv, r_send, r_recv, f_send, f_recv, tp_send, tp_recv, rp_send, rp_recv, out_sem,
    s_send, s_recv,
):
    x = lax.axis_index("grp")
    p = lax.axis_index("patch")
    c = p % 2
    y = (p // 2) % 4
    z = p // 8
    a = jnp.where(c == 0, z, x)
    m = jnp.where(c == 0, x, y)
    b = jnp.where(c == 0, y, z)
    npatch = 32
    u = (u0, u1, u2, u3, u4, u5, u6)
    line = c * 64 + a * 16
    plane = line + m * 4
    place = plane + b
    right = (p + 1) % npatch
    left = (p + npatch - 1) % npatch
    partner = p + 1 - 2 * c

    def device(last, middle, first):
        last, middle, first = last % 4, middle % 4, first % 4
        far = jnp.where(c == 0, last, first) * 8 + jnp.where(c == 0, first, middle) * 2 + c
        return (jnp.where(c == 0, middle, last), far)

    firsts = [device(a, m, b + d) for d in (1, 2, 3)]
    grps = [device(a, m + d, b) for d in (1, 2, 3)]
    lasts = [device(a + d, m, b) for d in (1, 2, 3)]
    other = (x, partner)

    own_f = pltpu.make_async_copy(f_hbm, fext.at[pl.ds(8, ROWS)], local_sem.at[0])
    own_cells = [
        pltpu.make_async_copy(ref, cells.at[n, pl.ds(8, ROWS)], local_sem.at[1 + n])
        for n, ref in enumerate((s_hbm, r_hbm, v_hbm))
    ]
    own_row = pltpu.make_async_copy(s_hbm.at[pl.ds(ROWS - 1, 1)], rows.at[place], local_sem.at[4])
    quarter = norms.shape[0]
    own_p = [
        pltpu.make_async_copy(coeffs_hbm.at[:, pl.ds(x * quarter, quarter)], coeffs, local_sem.at[5]),
        pltpu.make_async_copy(scales_hbm.at[pl.ds(x * quarter, quarter)], scales, local_sem.at[6]),
    ]
    own_t = [
        pltpu.make_async_copy(owners_hbm, owners, local_sem.at[7]),
        pltpu.make_async_copy(adjacent_hbm, adjacent, local_sem.at[8]),
    ]
    for copy in own_cells + [own_f, own_row] + own_t + own_p:
        copy.start()

    barrier = pltpu.get_barrier_semaphore()
    peers = [(x, left), (x, right)] + firsts + grps + lasts + [other]
    for peer in peers:
        pl.semaphore_signal(barrier, inc=1, device_id=peer, device_id_type=MESH)

    side = lax.broadcasted_iota(jnp.int32, (2 * Z, 2 * Z), 0)
    lanes = lax.broadcasted_iota(jnp.int32, (2 * Z, 2 * Z), 1)
    cell = 2 * (lanes & 63) + (lanes >> 7)
    same_cell = (side & 127) == cell
    shuffle[...] = jnp.where(same_cell & ((side >> 7) == ((lanes >> 6) & 1)), 1.0, 0.0).astype(jnp.bfloat16)
    split[...] = jnp.where(same_cell[0:Z], 1.0, 0.0)
    for copy in own_t:
        copy.wait()
    found[...] = jnp.zeros_like(found)
    count = jnp.zeros((1, Z), jnp.int32)
    picked = [count, count]
    for n in range(owners.shape[0]):
        mine = jnp.where(owners[pl.ds(n, 1), :] == p, 1, 0)
        entry = adjacent[pl.ds(n, 1), :] + 1
        for k in range(2):
            picked[k] = picked[k] + jnp.where(count == k, mine * entry, 0)
        count = count + mine
    for k in range(2):
        found[pl.ds(k, 1), :] = picked[k] - 1
    pl.semaphore_wait(barrier, len(peers))

    def remote(src, dst, ssem, rsem, device):
        return pltpu.make_async_remote_copy(
            src_ref=src, dst_ref=dst, send_sem=ssem, recv_sem=rsem, device_id=device, device_id_type=MESH
        )

    to_left, to_right = [], []
    for n, ref in enumerate((s_hbm, r_hbm, v_hbm)):
        to_left.append(
            remote(ref.at[pl.ds(0, 8)], cells.at[n, pl.ds(8 + ROWS, 8)], halo_send.at[0, n], halo_recv.at[0, n], (x, left))
        )
        to_right.append(
            remote(ref.at[pl.ds(ROWS - 8, 8)], cells.at[n, pl.ds(0, 8)], halo_send.at[1, n], halo_recv.at[1, n], (x, right))
        )
    to_left.append(
        remote(f_hbm.at[pl.ds(0, HALO)], fext.at[pl.ds(8 + ROWS, HALO)], halo_send.at[0, 3], halo_recv.at[0, 3], (x, left))
    )
    to_right.append(
        remote(f_hbm.at[pl.ds(ROWS - HALO, HALO)], fext.at[pl.ds(8 - HALO, HALO)], halo_send.at[1, 3], halo_recv.at[1, 3], (x, right))
    )
    for copy in to_left:
        copy.start()
    for copy in to_right:
        copy.start()

    def stage1(buf, ssem, rsem):
        return [remote(buf.at[place], buf.at[place], ssem.at[0, n], rsem.at[0, n], dev) for n, dev in enumerate(firsts)]

    def stage2(buf, ssem, rsem):
        return [remote(buf.at[pl.ds(plane, 4)], buf.at[pl.ds(plane, 4)], ssem.at[1, n], rsem.at[1, n], dev) for n, dev in enumerate(grps)]

    def stage3(buf, ssem, rsem):
        return [remote(buf.at[pl.ds(line, 16)], buf.at[pl.ds(line, 16)], ssem.at[2, n], rsem.at[2, n], dev) for n, dev in enumerate(lasts)]

    def start(copies):
        for copy in copies:
            copy.start()

    own_row.wait()
    r1 = stage1(rows, r_send, r_recv)
    start(r1)

    lane = lax.broadcasted_iota(jnp.int32, (8, Z), 1)
    sub = lax.broadcasted_iota(jnp.int32, (8, Z), 0)

    def coefficients(e0):
        mid = cells[0, pl.ds(e0, 8), :]
        row = sub + e0
        keep_w = jnp.where((row == 8) & (p == 0), 0.0, 1.0)
        keep_e = jnp.where((row == 7 + ROWS) & (p == npatch - 1), 0.0, 1.0)
        keep_s = jnp.where(lane == 0, 0.0, 1.0)
        keep_n = jnp.where(lane == Z - 1, 0.0, 1.0)
        west = 0.5 * (mid + keep_w * cells[0, pl.ds(e0 - 1, 8), :])
        east = 0.5 * (mid + keep_e * cells[0, pl.ds(e0 + 1, 8), :])
        south = 0.5 * (mid + keep_s * pltpu.roll(mid, 1, 1))
        north = 0.5 * (mid + keep_n * pltpu.roll(mid, Z - 1, 1))
        volume = cells[2, pl.ds(e0, 8), :]
        rest = cells[1, pl.ds(e0, 8), :] + west + east + south + north
        diagonal = rest + volume
        weight = OMEGA / diagonal
        values = (
            1.0 - weight * rest,
            1.0 - weight * (rest + 3.0 * volume),
            weight * west * keep_w,
            weight * east * keep_e,
            weight * south * keep_s,
            weight * north * keep_n,
            weight * (1.0 / 3.0),
        )
        parted = lax.dot_general(
            jnp.concatenate(values, axis=0), split[...], (((1,), (0,)), ((), ())),
            precision=lax.Precision.HIGHEST, preferred_element_type=jnp.float32,
        )
        small[...] = parted
        for n in range(7):
            for parity in range(2):
                kind = 9 - n if n in (4, 5) and parity == 0 else n
                for k in range(8):
                    row = small[pl.ds(8 * n + k, 1), Z * parity : Z * parity + Z]
                    coef[kind, e0 + k, parity] = jnp.broadcast_to(row, (8, Z))

    half = 3 * K // 2
    plain = (((1,), (0,)), ((), ()))
    contract = (((1,), (1,)), ((), ()))

    def product(left_side, right_side, dims=contract):
        return lax.dot_general(left_side, right_side, dims, preferred_element_type=jnp.float32)

    def block(m, parity):
        return pl.ds(8 * m + 4 * parity, 4)

    def first_level(e, slot):
        value = fext[e]
        parted = product(jnp.concatenate([value[0:half], value[half:]], axis=1), shuffle[...], plain)
        for parity in range(2):
            spread[slot, parity] = parted[:, Z * parity : Z * parity + Z]
        for parity in range(2):
            parts = [spread[slot, parity, pl.ds(n, K // 2, stride=3), :].reshape(4, 8, Z) for n in range(3)]
            weight = coef[6, e, parity][None]
            total = parts[0] + parts[1] + parts[2]
            u0[e, block(0, parity)] = weight * total
            u0[e, block(1, parity)] = weight * (3.0 * parts[0] - total)
            u0[e, block(2, parity)] = weight * (3.0 * parts[1] - total)

    def first_levels(e0, n):
        def four(i, carry):
            for k in range(4):
                first_level(e0 + 4 * i + k, k)
            return carry

        lax.fori_loop(0, n // 4, four, 0)

    def turned(value, shift):
        return pltpu.roll(value.reshape(K // 2, Z), shift, 1).reshape(4, 8, Z)

    def update(e, m, parity, before, now, after, beside):
        centre = coef[1 if m == 0 else 0, e, parity][None]
        return (
            u0[e, block(m, parity)]
            + coef[2, e, parity][None] * before
            + coef[3, e, parity][None] * after
        ) + (
            centre * now
            + (coef[4, e, parity][None] * beside + coef[5, e, parity][None] * turned(beside, 1 if parity == 0 else Z - 1))
        )

    def sweep(level, e0, n):
        below, mine = u[level - 2], u[level - 1]
        for m in range(3):
            for parity in range(2):
                part = block(m, parity)
                before = below[e0 - 1, part]
                now = below[e0, part]
                for k in range(n):
                    after = below[e0 + k + 1, part]
                    beside = below[e0 + k, block(m, 1 - parity)]
                    mine[e0 + k, part] = update(e0 + k, m, parity, before, now, after, beside)
                    before, now = now, after

    def last_modes(e, count):
        result = []
        for m in range(count):
            both = []
            for parity in range(2):
                part = block(m, parity)
                beside = u6[e, block(m, 1 - parity)]
                both.append(update(e, m, parity, u6[e - 1, part], u6[e, part], u6[e + 1, part], beside))
            result.append(both)
        return result

    def emit(e, slot):
        total, first, second = last_modes(e, 3)
        for parity in range(2):
            t, f, g = total[parity], first[parity], second[parity]
            for n, value in enumerate((t + f, t + g, t - f - g)):
                spread[slot, parity, pl.ds(n, K // 2, stride=3), :] = value.reshape(K // 2, Z)
        value = jnp.concatenate([spread[slot, 0], spread[slot, 1]], axis=1).astype(jnp.bfloat16)
        joined = product(value, shuffle[...]).astype(jnp.bfloat16)
        out[e - 8, 0:half] = joined[:, 0:Z]
        out[e - 8, half:] = joined[:, Z:]

    for copy in own_cells:
        copy.wait()
    for e0 in (9, 17, 25, 31):
        coefficients(e0)
    own_f.wait()

    first_levels(8, ROWS)
    for level in range(2, 8):
        eights, fours = divmod((32 - 2 * level + 3) // 4, 2)

        def eight(i, carry, level=level):
            sweep(level, 8 + level + 8 * i, 8)
            return carry

        lax.fori_loop(0, eights, eight, 0)
        if fours:
            sweep(level, 8 + level + 8 * eights, 4)

    def finish(copies):
        for copy in copies:
            copy.wait_recv()

    finish(r1)
    r2 = stage2(rows, r_send, r_recv)
    start(r2)

    finish(to_left)
    coefficients(39)

    first_levels(39, 8)
    for level in range(2, 8):
        sweep(level, 40 - level, 8)
    total, first = last_modes(7 + ROWS, 2)
    ends = [(total[parity] + first[parity]).reshape(K // 2, Z).astype(jnp.bfloat16) for parity in range(2)]
    trace = product(jnp.concatenate(ends, axis=1), shuffle[...]).astype(jnp.bfloat16)
    traces[place, 0 : K // 2] = trace[:, 0:Z]
    traces[place, K // 2 :] = trace[:, Z:]
    finish(r2)
    r3 = stage3(rows, r_send, r_recv)
    start(r3)
    plane_of = {
        (dm, db): remote(
            traces.at[place], traces.at[place], t_send.at[dm, db], t_recv.at[dm, db], device(a, m + dm, b + db)
        )
        for dm in (2, 1, 3, 0)
        for db in (2, 1, 3, 0)
        if dm or db
    }
    start(plane_of.values())

    finish(to_right)
    coefficients(1)

    first_levels(1, 8)
    for level in range(2, 8):
        sweep(level, level, 8)

    def part(back, k):
        return traces.at[pl.ds(c * 64 + (a + 4 - back) % 4 * 16 + (m + k) % 4 * 4, 4)]

    def share(back, k):
        return remote(part(back, k), part(back, k), tp_send.at[back, k], tp_recv.at[back, k], other)

    ahead_of = [remote(part(0, k), part(0, k), f_send.at[0, k], f_recv.at[0, k], lasts[0]) for k in range(4)]
    behind_of = [remote(part(0, k), part(0, k), f_send.at[1, k], f_recv.at[1, k], lasts[2]) for k in range(4)]
    twice = [
        remote(part(1, 0), part(1, 0), f_send.at[2, 0], f_recv.at[2, 0], lasts[0]),
        remote(part(3, 1), part(3, 1), f_send.at[2, 1], f_recv.at[2, 1], lasts[2]),
        remote(part(0, 2), part(0, 2), f_send.at[2, 2], f_recv.at[2, 2], lasts[1]),
        remote(part(0, 3), part(0, 3), f_send.at[2, 3], f_recv.at[2, 3], lasts[1]),
    ]
    tp = [[share(back, k) for k in range(4)] for back in range(4)]

    def spread_out(k):
        for db in range(4):
            if k or db:
                plane_of[(4 - k) % 4, db].wait_recv()
        if k >= 2:
            twice[k].start()
        ahead_of[k].start()
        behind_of[k].start()
        tp[0][k].start()

    def pass_on(k):
        ahead_of[k].wait_recv()
        if k == 0:
            twice[k].start()
        behind_of[k].wait_recv()
        if k == 1:
            twice[k].start()
        tp[1][k].start()
        tp[3][k].start()

    spread_out(0)
    finish(r3)
    rp = remote(rows.at[pl.ds(c * 64, 64)], rows.at[pl.ds(c * 64, 64)], rp_send, rp_recv, other)
    rp.start()

    def four_emit(i, carry):
        for k in range(4):
            emit(8 + 4 * i + k, k)
        return carry

    quarters = []

    def emit_quarter(n):
        lax.fori_loop(2 * n, 2 * n + 2, four_emit, 0)
        rows_out = pl.ds(8 * n, 8)
        copy = pltpu.make_async_copy(out.at[rows_out], basis_hbm.at[rows_out], out_sem.at[n])
        copy.start()
        quarters.append(copy)

    emit_quarter(0)
    spread_out(1)
    spread_out(3)
    spread_out(2)
    emit_quarter(1)
    pass_on(0)
    emit_quarter(2)
    pass_on(1)
    emit_quarter(3)
    pass_on(3)
    pass_on(2)

    to_table = pltpu.make_async_copy(found, table, local_sem.at[9])
    to_table.start()
    for copy in own_p:
        copy.wait()
    scales_t[...] = scales[...].T
    narrow = coeffs[...].astype(jnp.bfloat16)
    weights[...] = narrow
    weights2[...] = jnp.zeros_like(weights2)
    weights2[0:K, 0:quarter] = narrow
    weights2[K:, quarter:] = narrow
    to_table.wait()

    for k in (0, 1, 3, 2):
        twice[k].wait_recv()
        tp[2][k].start()
    rp.wait_recv()
    for copies in tp:
        finish(copies)

    def pick(i, k):
        return jnp.maximum(table[k, i], 0)

    def blocks(n, forward, backward):
        for q in range(4):
            i = 4 * n + q
            where = position(i)
            scaled = (traces[where].astype(jnp.float32) * rows[where]).astype(jnp.bfloat16)
            pair = jnp.concatenate([traces[position(pick(i, 0))], traces[position(pick(i, 1))]], axis=0)
            forward[K * q : K * q + K] = product(scaled, pair).astype(jnp.bfloat16)
            backward[2 * K * q : 2 * K * q + 2 * K] = product(pair, scaled).astype(jnp.bfloat16)

    def residuals(n, forward, backward):
        ahead = product(forward[...], weights2[...], plain)
        behind = product(backward[...], weights[...], plain)
        for q in range(4):
            i = 4 * n + q
            own = scales_t[pl.ds(i, 1), :]
            for k in range(2):
                slot = 2 * i + k
                beside = scales_t[pl.ds(pick(i, k), 1), :]
                residual = (
                    own * ahead[K * q : K * q + K, quarter * k : quarter * k + quarter]
                    - beside * behind[2 * K * q + K * k : 2 * K * q + K * k + K]
                )
                part = jnp.sum((residual * residual).reshape(8, 8, quarter), axis=0)
                parts[pl.ds(pl.multiple_of(8 * slot, 8), 8), :] = jnp.where(table[k, i] >= 0, part, 0.0)

    chunks = traces.shape[0] // 4
    blocks(0, fw0, bw0)

    def two(i, carry):
        blocks(2 * i + 1, fw1, bw1)
        residuals(2 * i, fw0, bw0)
        blocks(jnp.minimum(2 * i + 2, chunks - 1), fw0, bw0)
        residuals(2 * i + 1, fw1, bw1)
        return carry

    lax.fori_loop(0, chunks // 2, two, 0)
    slots = norms.shape[1]
    squares = parts[pl.ds(0, slots, stride=8), :]
    for n in range(1, 8):
        squares = squares + parts[pl.ds(n, slots, stride=8), :]
    inbox[p] = jnp.sum(squares, axis=0, keepdims=True)
    norms[...] = jnp.sqrt(squares.T + EPS)
    shares = [
        remote(inbox.at[p], inbox.at[p], s_send.at[d - 1], s_recv.at[d - 1], (x, (p + d) % npatch))
        for d in range(1, npatch)
    ]
    start(shares)
    finish(shares)
    total = inbox[0]
    for n in range(1, npatch):
        total = total + inbox[n]
    estimate[...] = jnp.sqrt(total + EPS)
    for copy in to_left + to_right + r1 + r2 + r3 + [rp] + list(plane_of.values()) + ahead_of + behind_of + twice + sum(tp, []) + shares:
        copy.wait_send()
    for copy in quarters:
        copy.wait()


def body(forcing, stiffness, reaction, volumetric, adjacency, owner_map, param_scale, coefficients):
    anywhere = pl.BlockSpec(memory_space=pl.ANY)
    vmem = pl.BlockSpec(memory_space=pltpu.VMEM)
    dma = pltpu.SemaphoreType.DMA
    f32, bf16 = jnp.float32, jnp.bfloat16
    slots = 2 * owner_map.shape[0]
    quarter = param_scale.shape[0] // lax.axis_size("grp")
    npatch = lax.axis_size("patch")
    basis, norms, estimate = pl.pallas_call(
        round_kernel,
        name="round",
        out_shape=(
            jax.ShapeDtypeStruct((ROWS, 3 * K, Z), bf16),
            jax.ShapeDtypeStruct((quarter, slots), f32),
            jax.ShapeDtypeStruct((1, quarter), f32),
        ),
        in_specs=[anywhere] * 8,
        out_specs=(anywhere, vmem, vmem),
        scratch_shapes=[pltpu.VMEM((48, 24, 8, Z), f32)] * 7
        + [
            pltpu.VMEM((48, 3 * K, Z), bf16),
            pltpu.VMEM((3, 48, Z), f32),
            pltpu.VMEM((56, 2 * Z), f32),
            pltpu.VMEM((7, 48, 2, 8, Z), f32),
            pltpu.VMEM((4, 2, 3 * K // 2, Z), f32),
            pltpu.VMEM((ROWS, 3 * K, Z), bf16),
            pltpu.VMEM((128, K, Z), bf16),
            pltpu.VMEM((128, 1, Z), f32),
            pltpu.VMEM(owner_map.T.shape, jnp.int32),
            pltpu.VMEM(owner_map.T.shape, jnp.int32),
            pltpu.VMEM((8, Z), jnp.int32),
            pltpu.SMEM((8, Z), jnp.int32),
            pltpu.VMEM((2 * Z, 2 * Z), bf16),
            pltpu.VMEM((Z, 2 * Z), f32),
            pltpu.VMEM((K, quarter), f32),
            pltpu.VMEM((quarter, 128), f32),
            pltpu.VMEM((128, quarter), f32),
            pltpu.VMEM((K, quarter), bf16),
            pltpu.VMEM((2 * K, 2 * quarter), bf16),
            pltpu.VMEM((4 * K, 2 * K), bf16),
            pltpu.VMEM((8 * K, K), bf16),
            pltpu.VMEM((4 * K, 2 * K), bf16),
            pltpu.VMEM((8 * K, K), bf16),
            pltpu.VMEM((8 * slots, quarter), f32),
            pltpu.VMEM((npatch, 1, quarter), f32),
            dma((10,)),
            dma((2, 4)),
            dma((2, 4)),
            dma((4, 4)),
            dma((4, 4)),
            dma((3, 3)),
            dma((3, 3)),
            dma((3, 4)),
            dma((3, 4)),
            dma((4, 4)),
            dma((4, 4)),
            dma,
            dma,
            dma((4,)),
            dma((npatch - 1,)),
            dma((npatch - 1,)),
        ],
        compiler_params=pltpu.CompilerParams(collective_id=0, has_side_effects=True, vmem_limit_bytes=VMEM_LIMIT),
    )(
        forcing[0], stiffness[0], reaction[0], volumetric[0], coefficients.T, param_scale, owner_map.T, adjacency.T
    )
    return (basis[None], norms[None], estimate[0])


def solution(mesh):
    placed = (
        P("grp", "patch", None, None),
        P("grp", "patch", None),
        P("grp", "patch", None),
        P("grp", "patch", None),
        P(),
        P(),
        P(),
        P(),
    )
    return jax.shard_map(
        body,
        mesh=mesh,
        in_specs=placed,
        out_specs=(P("grp", "patch", None, None), P("patch", "grp", None), P("grp")),
        check_vma=False,
    )
```

```python
import jax
import jax.numpy as jnp
from jax import lax
from jax.experimental import pallas as pl
from jax.experimental.pallas import tpu as pltpu
from jax.sharding import PartitionSpec as P

MESH = pl.DeviceIdType.MESH
OMEGA = 0.8
EPS = 1e-06
ROWS = 32
K = 64
Z = 128
HALO = 7
VMEM_LIMIT = 62 * 1024 * 1024


def position(i):
    core = i & 1
    y = (i >> 1) & 3
    z = (i >> 3) & 3
    x = i >> 5
    return core * 64 + jnp.where(core == 0, z * 16 + x * 4 + y, x * 16 + y * 4 + z)


def round_kernel(
    f_hbm, s_hbm, r_hbm, v_hbm, coeffs_hbm, scales_hbm, owners_hbm, adjacent_hbm,
    out, norms, estimate,
    u0, u1, u2, u3, u4, u5, u6,
    fext, cells, small, coef, spread, traces, rows,
    owners, adjacent, found, table, shuffle, split, coeffs, scales, scales_t, weights, weights2, fw0, bw0, fw1, bw1, parts, inbox,
    local_sem, halo_send, halo_recv, t_send, t_recv, r_send, r_recv, f_send, f_recv, tp_send, tp_recv, rp_send, rp_recv,
    s_send, s_recv,
):
    x = lax.axis_index("grp")
    p = lax.axis_index("patch")
    c = p % 2
    y = (p // 2) % 4
    z = p // 8
    a = jnp.where(c == 0, z, x)
    m = jnp.where(c == 0, x, y)
    b = jnp.where(c == 0, y, z)
    npatch = 32
    u = (u0, u1, u2, u3, u4, u5, u6)
    line = c * 64 + a * 16
    plane = line + m * 4
    place = plane + b
    right = (p + 1) % npatch
    left = (p + npatch - 1) % npatch
    partner = p + 1 - 2 * c

    def device(last, middle, first):
        last, middle, first = last % 4, middle % 4, first % 4
        far = jnp.where(c == 0, last, first) * 8 + jnp.where(c == 0, first, middle) * 2 + c
        return (jnp.where(c == 0, middle, last), far)

    firsts = [device(a, m, b + d) for d in (1, 2, 3)]
    grps = [device(a, m + d, b) for d in (1, 2, 3)]
    lasts = [device(a + d, m, b) for d in (1, 2, 3)]
    other = (x, partner)

    own_f = pltpu.make_async_copy(f_hbm, fext.at[pl.ds(8, ROWS)], local_sem.at[0])
    own_cells = [
        pltpu.make_async_copy(ref, cells.at[n, pl.ds(8, ROWS)], local_sem.at[1 + n])
        for n, ref in enumerate((s_hbm, r_hbm, v_hbm))
    ]
    own_row = pltpu.make_async_copy(s_hbm.at[pl.ds(ROWS - 1, 1)], rows.at[place], local_sem.at[4])
    quarter = norms.shape[0]
    own_p = [
        pltpu.make_async_copy(coeffs_hbm.at[:, pl.ds(x * quarter, quarter)], coeffs, local_sem.at[5]),
        pltpu.make_async_copy(scales_hbm.at[pl.ds(x * quarter, quarter)], scales, local_sem.at[6]),
    ]
    own_t = [
        pltpu.make_async_copy(owners_hbm, owners, local_sem.at[7]),
        pltpu.make_async_copy(adjacent_hbm, adjacent, local_sem.at[8]),
    ]
    for copy in own_cells + [own_f, own_row] + own_t + own_p:
        copy.start()

    barrier = pltpu.get_barrier_semaphore()
    peers = [(x, left), (x, right)] + firsts + grps + lasts + [other]
    for peer in peers:
        pl.semaphore_signal(barrier, inc=1, device_id=peer, device_id_type=MESH)

    side = lax.broadcasted_iota(jnp.int32, (2 * Z, 2 * Z), 0)
    lanes = lax.broadcasted_iota(jnp.int32, (2 * Z, 2 * Z), 1)
    cell = 2 * (lanes & 63) + (lanes >> 7)
    same_cell = (side & 127) == cell
    shuffle[...] = jnp.where(same_cell & ((side >> 7) == ((lanes >> 6) & 1)), 1.0, 0.0).astype(jnp.bfloat16)
    split[...] = jnp.where(same_cell[0:Z], 1.0, 0.0)
    for copy in own_t:
        copy.wait()
    found[...] = jnp.zeros_like(found)
    count = jnp.zeros((1, Z), jnp.int32)
    picked = [count, count]
    for n in range(owners.shape[0]):
        mine = jnp.where(owners[pl.ds(n, 1), :] == p, 1, 0)
        entry = adjacent[pl.ds(n, 1), :] + 1
        for k in range(2):
            picked[k] = picked[k] + jnp.where(count == k, mine * entry, 0)
        count = count + mine
    for k in range(2):
        found[pl.ds(k, 1), :] = picked[k] - 1
    pl.semaphore_wait(barrier, len(peers))

    def remote(src, dst, ssem, rsem, device):
        return pltpu.make_async_remote_copy(
            src_ref=src, dst_ref=dst, send_sem=ssem, recv_sem=rsem, device_id=device, device_id_type=MESH
        )

    to_left, to_right = [], []
    for n, ref in enumerate((s_hbm, r_hbm, v_hbm)):
        to_left.append(
            remote(ref.at[pl.ds(0, 8)], cells.at[n, pl.ds(8 + ROWS, 8)], halo_send.at[0, n], halo_recv.at[0, n], (x, left))
        )
        to_right.append(
            remote(ref.at[pl.ds(ROWS - 8, 8)], cells.at[n, pl.ds(0, 8)], halo_send.at[1, n], halo_recv.at[1, n], (x, right))
        )
    to_left.append(
        remote(f_hbm.at[pl.ds(0, HALO)], fext.at[pl.ds(8 + ROWS, HALO)], halo_send.at[0, 3], halo_recv.at[0, 3], (x, left))
    )
    to_right.append(
        remote(f_hbm.at[pl.ds(ROWS - HALO, HALO)], fext.at[pl.ds(8 - HALO, HALO)], halo_send.at[1, 3], halo_recv.at[1, 3], (x, right))
    )
    for copy in to_left:
        copy.start()
    for copy in to_right:
        copy.start()

    def stage1(buf, ssem, rsem):
        return [remote(buf.at[place], buf.at[place], ssem.at[0, n], rsem.at[0, n], dev) for n, dev in enumerate(firsts)]

    def stage2(buf, ssem, rsem):
        return [remote(buf.at[pl.ds(plane, 4)], buf.at[pl.ds(plane, 4)], ssem.at[1, n], rsem.at[1, n], dev) for n, dev in enumerate(grps)]

    def stage3(buf, ssem, rsem):
        return [remote(buf.at[pl.ds(line, 16)], buf.at[pl.ds(line, 16)], ssem.at[2, n], rsem.at[2, n], dev) for n, dev in enumerate(lasts)]

    def start(copies):
        for copy in copies:
            copy.start()

    own_row.wait()
    r1 = stage1(rows, r_send, r_recv)
    start(r1)

    lane = lax.broadcasted_iota(jnp.int32, (8, Z), 1)
    sub = lax.broadcasted_iota(jnp.int32, (8, Z), 0)

    def coefficients(e0):
        mid = cells[0, pl.ds(e0, 8), :]
        row = sub + e0
        keep_w = jnp.where((row == 8) & (p == 0), 0.0, 1.0)
        keep_e = jnp.where((row == 7 + ROWS) & (p == npatch - 1), 0.0, 1.0)
        keep_s = jnp.where(lane == 0, 0.0, 1.0)
        keep_n = jnp.where(lane == Z - 1, 0.0, 1.0)
        west = 0.5 * (mid + keep_w * cells[0, pl.ds(e0 - 1, 8), :])
        east = 0.5 * (mid + keep_e * cells[0, pl.ds(e0 + 1, 8), :])
        south = 0.5 * (mid + keep_s * pltpu.roll(mid, 1, 1))
        north = 0.5 * (mid + keep_n * pltpu.roll(mid, Z - 1, 1))
        volume = cells[2, pl.ds(e0, 8), :]
        rest = cells[1, pl.ds(e0, 8), :] + west + east + south + north
        diagonal = rest + volume
        weight = OMEGA / diagonal
        values = (
            1.0 - weight * rest,
            1.0 - weight * (rest + 3.0 * volume),
            weight * west * keep_w,
            weight * east * keep_e,
            weight * south * keep_s,
            weight * north * keep_n,
            weight * (1.0 / 3.0),
        )
        parted = lax.dot_general(
            jnp.concatenate(values, axis=0), split[...], (((1,), (0,)), ((), ())),
            precision=lax.Precision.HIGHEST, preferred_element_type=jnp.float32,
        )
        small[...] = parted
        for n in range(7):
            for parity in range(2):
                kind = 9 - n if n in (4, 5) and parity == 0 else n
                for k in range(8):
                    row = small[pl.ds(8 * n + k, 1), Z * parity : Z * parity + Z]
                    coef[kind, e0 + k, parity] = jnp.broadcast_to(row, (8, Z))

    half = 3 * K // 2
    plain = (((1,), (0,)), ((), ()))
    contract = (((1,), (1,)), ((), ()))

    def product(left_side, right_side, dims=contract):
        return lax.dot_general(left_side, right_side, dims, preferred_element_type=jnp.float32)

    def block(m, parity):
        return pl.ds(8 * m + 4 * parity, 4)

    def first_level(e, slot):
        value = fext[e]
        parted = product(jnp.concatenate([value[0:half], value[half:]], axis=1), shuffle[...], plain)
        for parity in range(2):
            spread[slot, parity] = parted[:, Z * parity : Z * parity + Z]
        for parity in range(2):
            parts = [spread[slot, parity, pl.ds(n, K // 2, stride=3), :].reshape(4, 8, Z) for n in range(3)]
            weight = coef[6, e, parity][None]
            total = parts[0] + parts[1] + parts[2]
            u0[e, block(0, parity)] = weight * total
            u0[e, block(1, parity)] = weight * (3.0 * parts[0] - total)
            u0[e, block(2, parity)] = weight * (3.0 * parts[1] - total)

    def first_levels(e0, n):
        def four(i, carry):
            for k in range(4):
                first_level(e0 + 4 * i + k, k)
            return carry

        lax.fori_loop(0, n // 4, four, 0)

    def turned(value, shift):
        return pltpu.roll(value.reshape(K // 2, Z), shift, 1).reshape(4, 8, Z)

    def update(e, m, parity, before, now, after, beside):
        centre = coef[1 if m == 0 else 0, e, parity][None]
        return (
            u0[e, block(m, parity)]
            + coef[2, e, parity][None] * before
            + coef[3, e, parity][None] * after
        ) + (
            centre * now
            + (coef[4, e, parity][None] * beside + coef[5, e, parity][None] * turned(beside, 1 if parity == 0 else Z - 1))
        )

    def sweep(level, e0, n):
        below, mine = u[level - 2], u[level - 1]
        for m in range(3):
            for parity in range(2):
                part = block(m, parity)
                before = below[e0 - 1, part]
                now = below[e0, part]
                for k in range(n):
                    after = below[e0 + k + 1, part]
                    beside = below[e0 + k, block(m, 1 - parity)]
                    mine[e0 + k, part] = update(e0 + k, m, parity, before, now, after, beside)
                    before, now = now, after

    def last_modes(e, count):
        result = []
        for m in range(count):
            both = []
            for parity in range(2):
                part = block(m, parity)
                beside = u6[e, block(m, 1 - parity)]
                both.append(update(e, m, parity, u6[e - 1, part], u6[e, part], u6[e + 1, part], beside))
            result.append(both)
        return result

    def emit(e, slot):
        total, first, second = last_modes(e, 3)
        for parity in range(2):
            t, f, g = total[parity], first[parity], second[parity]
            for n, value in enumerate((t + f, t + g, t - f - g)):
                spread[slot, parity, pl.ds(n, K // 2, stride=3), :] = value.reshape(K // 2, Z)
        value = jnp.concatenate([spread[slot, 0], spread[slot, 1]], axis=1).astype(jnp.bfloat16)
        joined = product(value, shuffle[...]).astype(jnp.bfloat16)
        out[e - 8, 0:half] = joined[:, 0:Z]
        out[e - 8, half:] = joined[:, Z:]

    for copy in own_cells:
        copy.wait()
    for e0 in (9, 17, 25, 31):
        coefficients(e0)
    own_f.wait()

    first_levels(8, ROWS)
    for level in range(2, 8):
        eights, fours = divmod((32 - 2 * level + 3) // 4, 2)

        def eight(i, carry, level=level):
            sweep(level, 8 + level + 8 * i, 8)
            return carry

        lax.fori_loop(0, eights, eight, 0)
        if fours:
            sweep(level, 8 + level + 8 * eights, 4)

    def finish(copies):
        for copy in copies:
            copy.wait_recv()

    finish(r1)
    r2 = stage2(rows, r_send, r_recv)
    start(r2)

    finish(to_left)
    coefficients(39)

    first_levels(39, 8)
    for level in range(2, 8):
        sweep(level, 40 - level, 8)
    total, first = last_modes(7 + ROWS, 2)
    ends = [(total[parity] + first[parity]).reshape(K // 2, Z).astype(jnp.bfloat16) for parity in range(2)]
    trace = product(jnp.concatenate(ends, axis=1), shuffle[...]).astype(jnp.bfloat16)
    traces[place, 0 : K // 2] = trace[:, 0:Z]
    traces[place, K // 2 :] = trace[:, Z:]
    finish(r2)
    r3 = stage3(rows, r_send, r_recv)
    start(r3)
    plane_of = {
        (dm, db): remote(
            traces.at[place], traces.at[place], t_send.at[dm, db], t_recv.at[dm, db], device(a, m + dm, b + db)
        )
        for dm in (2, 1, 3, 0)
        for db in (2, 1, 3, 0)
        if dm or db
    }
    start(plane_of.values())

    finish(to_right)
    coefficients(1)

    first_levels(1, 8)
    for level in range(2, 8):
        sweep(level, level, 8)

    def part(back, k):
        return traces.at[pl.ds(c * 64 + (a + 4 - back) % 4 * 16 + (m + k) % 4 * 4, 4)]

    def share(back, k):
        return remote(part(back, k), part(back, k), tp_send.at[back, k], tp_recv.at[back, k], other)

    ahead_of = [remote(part(0, k), part(0, k), f_send.at[0, k], f_recv.at[0, k], lasts[0]) for k in range(4)]
    behind_of = [remote(part(0, k), part(0, k), f_send.at[1, k], f_recv.at[1, k], lasts[2]) for k in range(4)]
    twice = [
        remote(part(1, 0), part(1, 0), f_send.at[2, 0], f_recv.at[2, 0], lasts[0]),
        remote(part(3, 1), part(3, 1), f_send.at[2, 1], f_recv.at[2, 1], lasts[2]),
        remote(part(0, 2), part(0, 2), f_send.at[2, 2], f_recv.at[2, 2], lasts[1]),
        remote(part(0, 3), part(0, 3), f_send.at[2, 3], f_recv.at[2, 3], lasts[1]),
    ]
    tp = [[share(back, k) for k in range(4)] for back in range(4)]

    def spread_out(k):
        for db in range(4):
            if k or db:
                plane_of[(4 - k) % 4, db].wait_recv()
        if k >= 2:
            twice[k].start()
        ahead_of[k].start()
        behind_of[k].start()
        tp[0][k].start()

    def pass_on(k):
        ahead_of[k].wait_recv()
        if k == 0:
            twice[k].start()
        behind_of[k].wait_recv()
        if k == 1:
            twice[k].start()
        tp[1][k].start()
        tp[3][k].start()

    spread_out(0)
    finish(r3)
    rp = remote(rows.at[pl.ds(c * 64, 64)], rows.at[pl.ds(c * 64, 64)], rp_send, rp_recv, other)
    rp.start()

    def four_emit(i, carry):
        for k in range(4):
            emit(8 + 4 * i + k, k)
        return carry

    def emit_quarter(n):
        lax.fori_loop(2 * n, 2 * n + 2, four_emit, 0)

    emit_quarter(0)
    spread_out(1)
    spread_out(3)
    spread_out(2)
    emit_quarter(1)
    pass_on(0)
    emit_quarter(2)
    pass_on(1)
    emit_quarter(3)
    pass_on(3)
    pass_on(2)

    to_table = pltpu.make_async_copy(found, table, local_sem.at[9])
    to_table.start()
    for copy in own_p:
        copy.wait()
    scales_t[...] = scales[...].T
    narrow = coeffs[...].astype(jnp.bfloat16)
    weights[...] = narrow
    weights2[...] = jnp.zeros_like(weights2)
    weights2[0:K, 0:quarter] = narrow
    weights2[K:, quarter:] = narrow
    to_table.wait()

    for k in (0, 1, 3, 2):
        twice[k].wait_recv()
        tp[2][k].start()
    rp.wait_recv()
    for copies in tp:
        finish(copies)

    def pick(i, k):
        return jnp.maximum(table[k, i], 0)

    def blocks(n, forward, backward):
        for q in range(4):
            i = 4 * n + q
            where = position(i)
            scaled = (traces[where].astype(jnp.float32) * rows[where]).astype(jnp.bfloat16)
            pair = jnp.concatenate([traces[position(pick(i, 0))], traces[position(pick(i, 1))]], axis=0)
            forward[K * q : K * q + K] = product(scaled, pair).astype(jnp.bfloat16)
            backward[2 * K * q : 2 * K * q + 2 * K] = product(pair, scaled).astype(jnp.bfloat16)

    def residuals(n, forward, backward):
        ahead = product(forward[...], weights2[...], plain)
        behind = product(backward[...], weights[...], plain)
        for q in range(4):
            i = 4 * n + q
            own = scales_t[pl.ds(i, 1), :]
            for k in range(2):
                slot = 2 * i + k
                beside = scales_t[pl.ds(pick(i, k), 1), :]
                residual = (
                    own * ahead[K * q : K * q + K, quarter * k : quarter * k + quarter]
                    - beside * behind[2 * K * q + K * k : 2 * K * q + K * k + K]
                )
                part = jnp.sum((residual * residual).reshape(8, 8, quarter), axis=0)
                parts[pl.ds(pl.multiple_of(8 * slot, 8), 8), :] = jnp.where(table[k, i] >= 0, part, 0.0)

    chunks = traces.shape[0] // 4
    blocks(0, fw0, bw0)

    def two(i, carry):
        blocks(2 * i + 1, fw1, bw1)
        residuals(2 * i, fw0, bw0)
        blocks(jnp.minimum(2 * i + 2, chunks - 1), fw0, bw0)
        residuals(2 * i + 1, fw1, bw1)
        return carry

    lax.fori_loop(0, chunks // 2, two, 0)
    slots = norms.shape[1]
    squares = parts[pl.ds(0, slots, stride=8), :]
    for n in range(1, 8):
        squares = squares + parts[pl.ds(n, slots, stride=8), :]
    inbox[p] = jnp.sum(squares, axis=0, keepdims=True)
    norms[...] = jnp.sqrt(squares.T + EPS)
    shares = [
        remote(inbox.at[p], inbox.at[p], s_send.at[d - 1], s_recv.at[d - 1], (x, (p + d) % npatch))
        for d in range(1, npatch)
    ]
    start(shares)
    finish(shares)
    total = inbox[0]
    for n in range(1, npatch):
        total = total + inbox[n]
    estimate[...] = jnp.sqrt(total + EPS)
    for copy in to_left + to_right + r1 + r2 + r3 + [rp] + list(plane_of.values()) + ahead_of + behind_of + twice + sum(tp, []) + shares:
        copy.wait_send()


def body(forcing, stiffness, reaction, volumetric, adjacency, owner_map, param_scale, coefficients):
    anywhere = pl.BlockSpec(memory_space=pltpu.HBM)
    vmem = pl.BlockSpec(memory_space=pltpu.VMEM)
    dma = pltpu.SemaphoreType.DMA
    f32, bf16 = jnp.float32, jnp.bfloat16
    slots = 2 * owner_map.shape[0]
    quarter = param_scale.shape[0] // lax.axis_size("grp")
    npatch = lax.axis_size("patch")
    basis, norms, estimate = pl.pallas_call(
        round_kernel,
        name="round",
        out_shape=(
            pltpu.VMEM((ROWS, 3 * K, Z), bf16),
            pltpu.VMEM((quarter, slots), f32),
            pltpu.VMEM((1, quarter), f32),
        ),
        in_specs=[anywhere] * 8,
        out_specs=(vmem, vmem, vmem),
        scratch_shapes=[pltpu.VMEM((48, 24, 8, Z), f32)] * 7
        + [
            pltpu.VMEM((48, 3 * K, Z), bf16),
            pltpu.VMEM((3, 48, Z), f32),
            pltpu.VMEM((56, 2 * Z), f32),
            pltpu.VMEM((7, 48, 2, 8, Z), f32),
            pltpu.VMEM((4, 2, 3 * K // 2, Z), f32),
            pltpu.VMEM((128, K, Z), bf16),
            pltpu.VMEM((128, 1, Z), f32),
            pltpu.VMEM(owner_map.T.shape, jnp.int32),
            pltpu.VMEM(owner_map.T.shape, jnp.int32),
            pltpu.VMEM((8, Z), jnp.int32),
            pltpu.SMEM((8, Z), jnp.int32),
            pltpu.VMEM((2 * Z, 2 * Z), bf16),
            pltpu.VMEM((Z, 2 * Z), f32),
            pltpu.VMEM((K, quarter), f32),
            pltpu.VMEM((quarter, 128), f32),
            pltpu.VMEM((128, quarter), f32),
            pltpu.VMEM((K, quarter), bf16),
            pltpu.VMEM((2 * K, 2 * quarter), bf16),
            pltpu.VMEM((4 * K, 2 * K), bf16),
            pltpu.VMEM((8 * K, K), bf16),
            pltpu.VMEM((4 * K, 2 * K), bf16),
            pltpu.VMEM((8 * K, K), bf16),
            pltpu.VMEM((8 * slots, quarter), f32),
            pltpu.VMEM((npatch, 1, quarter), f32),
            dma((10,)),
            dma((2, 4)),
            dma((2, 4)),
            dma((4, 4)),
            dma((4, 4)),
            dma((3, 3)),
            dma((3, 3)),
            dma((3, 4)),
            dma((3, 4)),
            dma((4, 4)),
            dma((4, 4)),
            dma,
            dma,
            dma((npatch - 1,)),
            dma((npatch - 1,)),
        ],
        compiler_params=pltpu.CompilerParams(collective_id=0, has_side_effects=True, vmem_limit_bytes=VMEM_LIMIT),
    )(
        forcing[0], stiffness[0], reaction[0], volumetric[0], coefficients.T, param_scale, owner_map.T, adjacency.T
    )
    return (basis[None], norms[None], estimate[0])


def solution(mesh):
    placed = (
        P("grp", "patch", None, None),
        P("grp", "patch", None),
        P("grp", "patch", None),
        P("grp", "patch", None),
        P(),
        P(),
        P(),
        P(),
    )
    return jax.shard_map(
        body,
        mesh=mesh,
        in_specs=placed,
        out_specs=(P("grp", "patch", None, None), P("patch", "grp", None), P("grp")),
        check_vma=False,
    )
```
